128 devices in a mesh: user: 4 (over y_lo, core), item: 32 (over z, y_hi, x).
Axes of the slice: x: 4, y: 4 (y_hi: 2, y_lo: 2; y = y_hi * 2 + y_lo), z: 4, core: 2. Of those that a mesh axis runs over, the one named last changes fastest.
Arguments:
- users: bfloat16 [4096, 256], P('user'), may hold values from -40 to 40
- catalog_vectors: bfloat16 [262144, 256], P('item'), may hold values from -8 to 8
- positives: int32 [4096], P('user'), may hold values from 0 to 262143
Outputs:
- loss: float32 [4096], P('user')
- user_grad: bfloat16 [4096, 256], P('user')
- item_grad: bfloat16 [262144, 256], P(('item', 'user'))
The draws below stay inside these ranges and needn't reach their ends.
All inputs are finite; a program needn't handle non-finite values.
Results may differ from the reference program's by a relative error of at most 0.0034.
Values may be sent and summed in bfloat16 or wider, within the bound.
No kernel may reach another device: no remote copies, remote signals or barrier semaphores. Data moves between devices by JAX's collectives and lax.ppermute only.
A program may use at most 64 MiB of HBM per device.

```python
import math
import jax
import jax.numpy as jnp
from jax import lax

E = 256
USER_DEV = 1024
USERS = 4096
ITEMS = 262144
N_USER = 4


def shared_draw(key):
    item_key = jax.random.fold_in(key, 11)
    user_key = jax.random.fold_in(key, 12)
    sign_key = jax.random.fold_in(key, 14)
    item_vals = jnp.clip(jax.random.normal(item_key, (ITEMS, E), jnp.float32), -6.0, 6.0)
    user_vals = jnp.clip(jax.random.normal(user_key, (USERS, E), jnp.float32), -6.0, 6.0)
    signs = jnp.where(jax.random.bernoulli(sign_key, 0.5, (6, E)), 1.0, -1.0).astype(jnp.float32)
    targets = [110.0, 160.0, 230.0, 110.0, 160.0, 230.0]
    for number in range(6):
        target_score = targets[number]
        item_row = number * (ITEMS // 7) % ITEMS
        partner = (item_row + 1) % ITEMS
        user_row = number * (USERS // 6) % USERS
        base_row = 2.0 * signs[number]
        item_vals = item_vals.at[item_row].set(base_row)
        item_vals = item_vals.at[partner].set(base_row * (1.0 - 2.5 / target_score))
        user_vals = user_vals.at[user_row].set(signs[number] * (target_score * 2.0 / E))
    return (user_vals, item_vals)


def draw_users(key, part):
    user_vals, item_vals = shared_draw(key)
    return user_vals.astype(jnp.bfloat16)


def draw_catalog_vectors(key, part):
    user_vals, item_vals = shared_draw(key)
    return item_vals.astype(jnp.bfloat16)


def place_ends(drawn, own_key, low, largest):
    longest = drawn.shape.index(max(drawn.shape))
    spots = []
    for shift in (0, 1):
        where = [jax.random.randint(jax.random.fold_in(own_key, axis), (), 0, length) for axis, length in enumerate(drawn.shape)]
        where[longest] = (where[longest] + shift) % drawn.shape[longest]
        spots.append(tuple(where))
    return drawn.at[spots[0]].set(low).at[spots[1]].set(largest)


def setup_inputs(seed: int = 0) -> dict:
    key_list = jax.random.split(jax.random.key(seed), 4)
    users = draw_users(jax.random.fold_in(key_list[3], 71), 0)
    catalog_vectors = draw_catalog_vectors(jax.random.fold_in(key_list[3], 71), 0)
    positives = place_ends(jax.random.randint(key_list[2], (USERS,), 0, ITEMS), jax.random.fold_in(key_list[2], 1), 0, ITEMS - 1).astype(jnp.int32)
    return {"users": users, "catalog_vectors": catalog_vectors, "positives": positives}


sharpness_divisor = 4.0


def reference(users, catalog_vectors, positives):
    count = catalog_vectors.shape[0]
    width = catalog_vectors.shape[1]
    row_block = math.gcd(USER_DEV, 256)
    item_index = lax.broadcasted_iota(jnp.int32, (1, count), 1)

    def shard_step(total, index):
        user_shard = lax.dynamic_slice_in_dim(users, (index * USER_DEV).astype(jnp.int32), USER_DEV, 0)
        pos_shard = lax.dynamic_slice_in_dim(positives, (index * USER_DEV).astype(jnp.int32), USER_DEV, 0)
        user_blocks = user_shard.reshape(USER_DEV // row_block, row_block, width)
        pos_blocks = pos_shard.reshape(USER_DEV // row_block, row_block)

        def row_step(accumulated_sum, inputs):
            customer_vector_list, pos_rows = inputs
            affinity_grid = jnp.dot(customer_vector_list, catalog_vectors.T, preferred_element_type=jnp.float32) / sharpness_divisor
            top = jnp.max(affinity_grid, axis=1)
            lse = top + jnp.log(jnp.sum(jnp.exp(affinity_grid - top[:, None]), axis=1))
            positive_indicator = item_index == pos_rows[:, None]
            pos_score = jnp.sum(jnp.where(positive_indicator, affinity_grid, 0.0), axis=1)
            normalized_probabilities = (jnp.exp(affinity_grid - lse[:, None]) - positive_indicator.astype(jnp.float32)).astype(jnp.bfloat16)
            customer_fraction = jnp.dot(normalized_probabilities, catalog_vectors, preferred_element_type=jnp.float32) / sharpness_divisor
            accumulated_sum = accumulated_sum + jnp.dot(normalized_probabilities.T, customer_vector_list, preferred_element_type=jnp.float32)
            return accumulated_sum, (lse - pos_score, customer_fraction.astype(jnp.bfloat16))

        accumulated_sum, (losses, user_parts) = lax.scan(row_step, jnp.zeros((count, width), jnp.float32), (user_blocks, pos_blocks))
        return total + accumulated_sum / sharpness_divisor, (losses.reshape(-1), user_parts.reshape(-1, width))

    total, (losses, user_parts) = lax.scan(shard_step, jnp.zeros((count, width), jnp.float32), jnp.arange(N_USER, dtype=jnp.int32))
    return losses.reshape(-1), user_parts.reshape(-1, width), total.astype(jnp.bfloat16)
```

```python
import functools
import math

import jax
import jax.numpy as jnp
from jax import lax
from jax.experimental import pallas as pl
from jax.experimental.pallas import tpu as pltpu
from jax.sharding import Mesh
from jax.sharding import PartitionSpec as P

sharpness_divisor = 4.0
SCALE = math.log2(math.e) / sharpness_divisor
NT = (((1,), (1,)), ((), ()))
ITEM = ("z", "y_hi", "x")
USER = ("y_lo", "core")


def exp_of(x):
    return jnp.exp2(x * SCALE)


def pass1_kernel(tile, rb, pos_ref, u_ref, cat_ref, acc_ref, hit_ref, st_ref, c_ref, m_ref, l_ref, sem):
    rows = u_ref.shape[0]
    count, width = cat_ref.shape
    n = count // tile
    copies = []
    for i in range(n):
        part = pl.ds(i * tile, tile)
        copies.append(pltpu.make_async_copy(cat_ref.at[part], c_ref.at[part], sem.at[i]))
        copies[-1].start()
    acc_ref[...] = jnp.zeros_like(acc_ref)
    hit_ref[...] = jnp.zeros_like(hit_ref)
    m_ref[...] = jnp.full_like(m_ref, -1e38)
    l_ref[...] = jnp.zeros_like(l_ref)
    for i in range(n):
        copies[i].wait()
        c = c_ref[i * tile : (i + 1) * tile]
        for b in range(rows // rb):
            sl = slice(b * rb, (b + 1) * rb)
            r = lax.dot_general(u_ref[sl], c, NT, preferred_element_type=jnp.float32)
            m_old = m_ref[sl]
            m_new = jnp.maximum(m_old, jnp.max(r, axis=1, keepdims=True))
            alpha = exp_of(m_old - m_new)
            m_ref[sl] = m_new
            total = l_ref[sl] * alpha
            ps = []
            for j in range(tile // 128):
                p = exp_of(r[:, j * 128 : (j + 1) * 128] - m_new)
                total = total + p
                ps.append(p.astype(jnp.bfloat16))
            l_ref[sl] = total
            wide = jnp.concatenate([alpha] * (width // 128), axis=1)
            acc_ref[sl] = acc_ref[sl] * wide + jnp.dot(
                jnp.concatenate(ps, axis=1), c, preferred_element_type=jnp.float32
            )

    @pl.loop(0, rows // 8)
    def _(g):
        here = [pos_ref[g * 8 + j] for j in range(8)]
        mine = [(h >= 0) & (h < count) for h in here]
        some = functools.reduce(jnp.logical_or, mine)

        @pl.when(some)
        def _():
            for j in range(8):

                @pl.when(mine[j])
                def _():
                    start = pl.multiple_of((here[j] >> 4) << 4, 16)
                    group = c_ref[pl.ds(start, 16), :].astype(jnp.float32)
                    inside = lax.broadcasted_iota(jnp.int32, group.shape, 0) == (here[j] & 15)
                    row = jnp.sum(jnp.where(inside, group, 0.0), axis=0, keepdims=True)
                    hit_ref[pl.ds(g * 8 + j, 1), :] = row

    for b in range(rows // 128):
        sl = slice(b * 128, (b + 1) * 128)
        total = jnp.sum(l_ref[sl], axis=1, keepdims=True)
        hit_score = jnp.sum(hit_ref[sl] * u_ref[sl].astype(jnp.float32), axis=1, keepdims=True)
        st_ref[0:1, sl] = m_ref[sl].T[0:1]
        st_ref[1:2, sl] = jnp.broadcast_to(total, (128, 128)).T[0:1]
        st_ref[2:3, sl] = jnp.broadcast_to(hit_score, (128, 128)).T[0:1]


def pass1(users, catalog, local_pos, tile=2048, rb=256):
    rows, width = users.shape
    count = catalog.shape[0]
    vmem = pl.BlockSpec(memory_space=pltpu.VMEM)
    return pl.pallas_call(
        functools.partial(pass1_kernel, tile, rb),
        in_specs=[pl.BlockSpec(memory_space=pltpu.SMEM), vmem, pl.BlockSpec(memory_space=pl.ANY)],
        out_specs=[vmem, vmem, vmem],
        out_shape=[
            jax.ShapeDtypeStruct((rows, width), jnp.float32),
            jax.ShapeDtypeStruct((rows, width), jnp.float32),
            jax.ShapeDtypeStruct((3, rows), jnp.float32),
        ],
        scratch_shapes=[
            pltpu.VMEM((count, width), jnp.bfloat16),
            pltpu.VMEM((rows, 128), jnp.float32),
            pltpu.VMEM((rows, 128), jnp.float32),
            pltpu.SemaphoreType.DMA((count // tile,)),
        ],
        cost_estimate=pl.CostEstimate(
            flops=4 * rows * count * width, bytes_accessed=2 * count * width, transcendentals=rows * count
        ),
        name="pass1",
    )(local_pos, users, catalog)


def pass2_kernel(tile, base_ref, c_ref, *refs):
    us, stats, out_ref = refs[:4], refs[4:8], refs[-1]
    first = base_ref[1] + pl.program_id(0) * tile
    c = c_ref[...]
    item = (lax.broadcasted_iota(jnp.int32, (tile, 128), 0) + first).astype(jnp.float32)
    total = jnp.zeros((tile, c.shape[1]), jnp.float32)
    for u_ref, st_ref in zip(us, stats):
        u = u_ref[...]
        r = lax.dot_general(c, u, NT, preferred_element_type=jnp.float32)
        ws = []
        for j in range(u.shape[0] // 128):
            sl = slice(j * 128, (j + 1) * 128)
            w = exp_of(r[:, sl] - st_ref[0:1, sl])
            w = jnp.where(st_ref[1:2, sl] == item, w - 1.0, w)
            ws.append(w.astype(jnp.bfloat16))
        total = total + jnp.dot(jnp.concatenate(ws, axis=1), u, preferred_element_type=jnp.float32)
    out_ref[...] = (total / sharpness_divisor).astype(out_ref.dtype)


def pass2(base, catalog, us, stats, items, part, parts, before, tile=512):
    rows, width = us[0].shape
    n = items // tile // parts
    lead = part * n
    resident = lambda i, b: (0, 0)
    in_specs = [pl.BlockSpec((tile, width), lambda i, b: (b[0] * (items // tile) + lead + i, 0))]
    in_specs += [pl.BlockSpec((rows, width), resident)] * 4
    in_specs += [pl.BlockSpec((2, rows), resident)] * 4
    args = [base + jnp.array([0, lead * tile], jnp.int32), catalog, *us, *stats]
    aliases = {}
    if before is not None:
        in_specs.append(pl.BlockSpec(memory_space=pl.ANY))
        aliases = {len(args): 0}
        args.append(before)
    return pl.pallas_call(
        functools.partial(pass2_kernel, tile),
        grid_spec=pltpu.PrefetchScalarGridSpec(
            num_scalar_prefetch=1,
            grid=(n,),
            in_specs=in_specs,
            out_specs=pl.BlockSpec((tile, width), lambda i, b: (lead + i, 0)),
        ),
        out_shape=jax.ShapeDtypeStruct((items, width), jnp.bfloat16),
        input_output_aliases=aliases,
        cost_estimate=pl.CostEstimate(
            flops=4 * rows * 4 * (items // parts) * width,
            bytes_accessed=2 * rows * 4 * width,
            transcendentals=rows * 4 * items // parts,
        ),
        name=f"pass2_{part}",
    )(*args)


def swap(x, axis, size, k):
    return lax.ppermute(x, axis, [(i, i ^ k) for i in range(size)])


def tree(a):
    return (a[0] + a[1]) + (a[2] + a[3]) if len(a) == 4 else a[0] + a[1]


def merge_stats(parts):
    top = functools.reduce(jnp.maximum, [p[0] for p in parts])
    total = tree([p[1] * exp_of(p[0] - top) for p in parts])
    return jnp.stack([top, total, tree([p[2] for p in parts])])


def gather_chunks(x, axis, size):
    mine = lax.axis_index(axis)
    got = jnp.stack([x] + [swap(x, axis, size, k) for k in range(1, size)])
    pieces = [lax.dynamic_index_in_dim(got, mine ^ k, keepdims=False) for k in range(size)]
    return jnp.concatenate(pieces, axis=0)


def scatter_sum(x, axis, size, dtype):
    mine = lax.axis_index(axis)
    chunks = x.reshape(size, x.shape[0] // size, x.shape[1])
    own = lax.dynamic_index_in_dim(chunks, mine, keepdims=False)
    others = []
    for k in range(1, size):
        piece = lax.dynamic_index_in_dim(chunks, mine ^ k, keepdims=False).astype(dtype)
        others.append(swap(piece, axis, size, k).astype(jnp.float32))
    return tree([own] + others)


def per_device(users, catalog, positives):
    rows = users.shape[0]
    count = catalog.shape[0]
    items = count // 4
    shard = lax.axis_index(ITEM)
    member = lax.axis_index(USER)
    us = [users] + [swap(users, USER, 4, k) for k in (1, 2, 3)]
    partial, hits, stats = pass1(users, catalog, positives - shard * count)
    all_stats = stats
    for axis, size in (("x", 4), ("z", 4), ("y_hi", 2)):
        all_stats = merge_stats([all_stats] + [swap(all_stats, axis, size, k) for k in range(1, size)])
    lse = all_stats[0] / sharpness_divisor + jnp.log(all_stats[1])
    loss = lse - all_stats[2] / sharpness_divisor
    lse4 = lse * sharpness_divisor

    mine = jnp.stack([lse4, positives.astype(jnp.float32)])
    infos = [mine] + [swap(mine, USER, 4, k) for k in (1, 2, 3)]
    base = jnp.stack([member, shard * count + member * items])
    item_grad = None
    parts = 4
    for part in range(parts):
        item_grad = pass2(base, catalog, us, infos, items, part, parts, item_grad)

    weight = exp_of(stats[0] - lse4)
    value = (partial * weight[:, None] - hits) / sharpness_divisor
    value = scatter_sum(value, "x", 4, jnp.bfloat16)
    value = scatter_sum(value, "z", 4, jnp.float32)
    value = tree([value, swap(value, "y_hi", 2, 1)]).astype(jnp.bfloat16)
    value = gather_chunks(value, "z", 4)
    user_grad = gather_chunks(value, "x", 4)
    return loss, user_grad, item_grad


def solution(mesh):
    grid = Mesh(mesh.devices.reshape(2, 2, 4, 2, 4), USER + ITEM)
    return jax.shard_map(
        per_device,
        mesh=grid,
        in_specs=(P(USER, None), P(ITEM, None), P(USER)),
        out_specs=(P(USER), P(USER, None), P(ITEM + USER, None)),
        check_vma=False,
    )
```

```python
import functools
import math

import jax
import jax.numpy as jnp
from jax import lax
from jax.experimental import pallas as pl
from jax.experimental.pallas import tpu as pltpu
from jax.sharding import Mesh
from jax.sharding import PartitionSpec as P

sharpness_divisor = 4.0
SCALE = math.log2(math.e) / sharpness_divisor
NT = (((1,), (1,)), ((), ()))
ITEM = ("z", "y_hi", "x")
USER = ("y_lo", "core")
VMEM = pl.BlockSpec(memory_space=pltpu.VMEM)
SMEM = pl.BlockSpec(memory_space=pltpu.SMEM)
f32 = jnp.float32
bf16 = jnp.bfloat16


def exp_of(x):
    return jnp.exp2(x * SCALE)


def struct(*shape, dtype=f32):
    return jax.ShapeDtypeStruct(shape, dtype)


def as_row(column):
    return jnp.broadcast_to(column, (128, 128)).T[0:1]


def as_column(row):
    return jnp.broadcast_to(row, (128, 128)).T


def pass1_kernel(tile, rb, pos_ref, me_ref, u_ref, cat_ref, *refs):
    out_refs, (st_ref, c_ref, acc_ref, hit_ref, m_ref, l_ref, sem) = refs[:4], refs[4:]
    rows = u_ref.shape[0]
    count, width = cat_ref.shape
    n = count // tile
    copies = []
    for i in range(n):
        part = pl.ds(i * tile, tile)
        copies.append(pltpu.make_async_copy(cat_ref.at[part], c_ref.at[part], sem.at[i]))
        copies[-1].start()
    acc_ref[...] = jnp.zeros_like(acc_ref)
    hit_ref[...] = jnp.zeros_like(hit_ref)
    m_ref[...] = jnp.full_like(m_ref, -1e38)
    l_ref[...] = jnp.zeros_like(l_ref)
    for i in range(n):
        copies[i].wait()
        c = c_ref[i * tile : (i + 1) * tile]
        for b in range(rows // rb):
            sl = slice(b * rb, (b + 1) * rb)
            r = lax.dot_general(u_ref[sl], c, NT, preferred_element_type=f32)
            m_old = m_ref[sl]
            m_new = jnp.maximum(m_old, jnp.max(r, axis=1, keepdims=True))
            alpha = exp_of(m_old - m_new)
            m_ref[sl] = m_new
            total = l_ref[sl] * alpha
            ps = []
            for j in range(tile // 128):
                p = exp_of(r[:, j * 128 : (j + 1) * 128] - m_new)
                total = total + p
                ps.append(p.astype(bf16))
            l_ref[sl] = total
            wide = jnp.concatenate([alpha] * (width // 128), axis=1)
            acc_ref[sl] = acc_ref[sl] * wide + jnp.dot(
                jnp.concatenate(ps, axis=1), c, preferred_element_type=f32
            )

    @pl.loop(0, rows // 8)
    def _(g):
        here = [pos_ref[g * 8 + j] for j in range(8)]
        mine = [(h >= 0) & (h < count) for h in here]
        some = functools.reduce(jnp.logical_or, mine)

        @pl.when(some)
        def _():
            for j in range(8):

                @pl.when(mine[j])
                def _():
                    start = pl.multiple_of((here[j] >> 4) << 4, 16)
                    group = c_ref[pl.ds(start, 16), :].astype(f32)
                    inside = lax.broadcasted_iota(jnp.int32, group.shape, 0) == (here[j] & 15)
                    row = jnp.sum(jnp.where(inside, group, 0.0), axis=0, keepdims=True)
                    hit_ref[pl.ds(g * 8 + j, 1), :] = row

    for b in range(rows // 128):
        sl = slice(b * 128, (b + 1) * 128)
        total = jnp.sum(l_ref[sl], axis=1, keepdims=True)
        acc_ref[sl] = acc_ref[sl] * (1.0 / total)
        hit_score = jnp.sum(hit_ref[sl] * u_ref[sl].astype(f32), axis=1, keepdims=True)
        part = slice(b % 2 * 128, b % 2 * 128 + 128)
        st_ref[b // 2 : b // 2 + 1, part] = m_ref[sl].T[0:1] + sharpness_divisor * jnp.log(as_row(total))
        st_ref[4 + b // 2 : 5 + b // 2, part] = as_row(hit_score)
    chunk = rows // 4
    for k, out_ref in enumerate(out_refs):
        part = pl.ds(pl.multiple_of((me_ref[0] ^ k) * chunk, chunk), chunk)
        out_ref[0:chunk] = acc_ref[part, :].astype(bf16)
        out_ref[chunk:] = hit_ref[part, :].astype(bf16)


def pass1(users, catalog, local_pos, me, tile=2048, rb=256):
    rows, width = users.shape
    count = catalog.shape[0]
    return pl.pallas_call(
        functools.partial(pass1_kernel, tile, rb),
        in_specs=[SMEM, SMEM, VMEM, pl.BlockSpec(memory_space=pl.ANY)],
        out_specs=[VMEM] * 5,
        out_shape=[struct(rows // 2, width, dtype=bf16)] * 4 + [struct(8, rows // 4)],
        scratch_shapes=[
            pltpu.VMEM((count, width), bf16),
            pltpu.VMEM((rows, width), f32),
            pltpu.VMEM((rows, width), f32),
            pltpu.VMEM((rows, 128), f32),
            pltpu.VMEM((rows, 128), f32),
            pltpu.SemaphoreType.DMA((count // tile,)),
        ],
        cost_estimate=pl.CostEstimate(
            flops=4 * rows * count * width, bytes_accessed=2 * count * width, transcendentals=rows * count
        ),
        name="pass1",
    )(local_pos, me, users, catalog)


def merge_kernel(me_ref, all_ref, p0, p1, p2, p3, i0, i1, i2, i3, loss_ref, w_ref):
    x, member, shard = me_ref[0], me_ref[1], me_ref[2]
    shards = all_ref.shape[0] // 4
    for k, (pos_ref, info_ref) in enumerate(zip((p0, p1, p2, p3), (i0, i1, i2, i3))):
        first = (member ^ k) * shards
        stats = all_ref[pl.ds(first, shards)]
        top = jnp.max(stats, axis=0)
        lse4 = top + sharpness_divisor * jnp.log(jnp.sum(exp_of(stats - top[None]), axis=0))
        info_ref[0:4] = lse4[0:4]
        info_ref[4:8] = pos_ref[...].astype(f32)
        if k == 0:
            loss_ref[...] = (lse4[0:4] - jnp.sum(stats, axis=0)[4:8]) / sharpness_divisor
    for k in range(4):
        mine = all_ref[member * shards + (shard ^ k), pl.ds(x, 1), :]
        w_ref[k : k + 1] = exp_of(mine - i0[pl.ds(x, 1), :])
    w_ref[4:8] = jnp.zeros_like(w_ref[4:8])


def merge(me, every, positions):
    width = every.shape[2]
    return pl.pallas_call(
        merge_kernel,
        in_specs=[SMEM] + [VMEM] * 5,
        out_specs=[VMEM] * 6,
        out_shape=[struct(8, width)] * 4 + [struct(4, width), struct(8, width)],
        name="merge",
    )(me, every, *positions)


def combine_kernel(w_ref, a0, a1, a2, a3, out_ref):
    chunk, width = out_ref.shape
    for h in range(chunk // 128):
        sl = slice(h * 128, (h + 1) * 128)
        low = slice(chunk + h * 128, chunk + (h + 1) * 128)
        total = jnp.zeros((128, width), f32)
        for k, a_ref in enumerate((a0, a1, a2, a3)):
            column = as_column(w_ref[k : k + 1, sl])
            wide = jnp.concatenate([column] * (width // 128), axis=1)
            total = total + wide * a_ref[sl].astype(f32) - a_ref[low].astype(f32)
        out_ref[sl] = (total / sharpness_divisor).astype(out_ref.dtype)


def combine(weights, parts):
    rows, width = parts[0].shape
    return pl.pallas_call(
        combine_kernel,
        in_specs=[VMEM] * 5,
        out_specs=VMEM,
        out_shape=struct(rows // 2, width, dtype=bf16),
        name="combine",
    )(weights, *parts)


def pass2_kernel(tile, base_ref, c_ref, *refs):
    us, infos, out_ref = refs[:4], refs[4:8], refs[-1]
    first = base_ref[1] + pl.program_id(0) * tile
    c = c_ref[...]
    item = (lax.broadcasted_iota(jnp.int32, (tile, 128), 0) + first).astype(f32)
    total = jnp.zeros((tile, c.shape[1]), f32)
    for u_ref, info_ref in zip(us, infos):
        u = u_ref[...]
        r = lax.dot_general(c, u, NT, preferred_element_type=f32)
        ws = []
        for j in range(u.shape[0] // 128):
            part = slice(j % 2 * 128, j % 2 * 128 + 128)
            w = exp_of(r[:, j * 128 : (j + 1) * 128] - info_ref[j // 2 : j // 2 + 1, part])
            hit = info_ref[4 + j // 2 : 5 + j // 2, part] == item
            ws.append(jnp.where(hit, w - 1.0, w).astype(bf16))
        total = total + jnp.dot(jnp.concatenate(ws, axis=1), u, preferred_element_type=f32)
    out_ref[...] = (total / sharpness_divisor).astype(out_ref.dtype)


def pass2(base, catalog, us, infos, items, start, stop, before, tile=512):
    rows, width = us[0].shape
    lead = start // tile
    n = (stop - start) // tile
    resident = lambda i, b: (0, 0)
    in_specs = [pl.BlockSpec((tile, width), lambda i, b: (b[0] * (items // tile) + lead + i, 0))]
    in_specs += [pl.BlockSpec((rows, width), resident)] * 4
    in_specs += [pl.BlockSpec((8, rows // 4), resident)] * 4
    args = [base + jnp.array([0, start], jnp.int32), catalog, *us, *infos]
    aliases = {}
    if before is not None:
        in_specs.append(pl.BlockSpec(memory_space=pl.ANY))
        aliases = {len(args): 0}
        args.append(before)
    return pl.pallas_call(
        functools.partial(pass2_kernel, tile),
        grid_spec=pltpu.PrefetchScalarGridSpec(
            num_scalar_prefetch=1,
            grid=(n,),
            in_specs=in_specs,
            out_specs=pl.BlockSpec((tile, width), lambda i, b: (lead + i, 0)),
        ),
        out_shape=struct(items, width, dtype=bf16),
        input_output_aliases=aliases,
        cost_estimate=pl.CostEstimate(
            flops=16 * rows * (stop - start) * width,
            bytes_accessed=8 * rows * width,
            transcendentals=4 * rows * (stop - start),
        ),
        name="pass2",
    )(*args)


def swap(x, axis, size, k):
    return lax.ppermute(x, axis, [(i, i ^ k) for i in range(size)])


def per_device(users, catalog, positives):
    rows = users.shape[0]
    count = catalog.shape[0]
    items = count // 4
    x, member, shard = lax.axis_index("x"), lax.axis_index(USER), lax.axis_index(ITEM)
    me = jnp.stack([x, member, shard])
    pos = positives.reshape(4, rows // 4)
    over = swap(users, USER, 4, 2)
    us = [users, swap(users, USER, 4, 1), over, swap(over, USER, 4, 1)]
    positions = [pos] + [swap(pos, USER, 4, k) for k in (1, 2, 3)]
    *pieces, stats = pass1(users, catalog, positives - shard * count, me)
    got = [pieces[0]] + [swap(pieces[k], "x", 4, k) for k in (1, 2, 3)]
    every = jnp.broadcast_to(stats[None], (128,) + stats.shape)
    every = lax.all_to_all(every, USER + ITEM, 0, 0, tiled=True)
    *infos, loss, weights = merge(me, every, positions)
    value = combine(weights, got)
    base = jnp.stack([member, shard * count + member * items])

    a = [value] + [swap(value, "z", 4, k) for k in (1, 2, 3)]
    item_grad = pass2(base, catalog, us, infos, items, 0, SPLIT[0], None)
    a = [v.astype(f32) for v in a]
    value = (a[0] + a[1]) + (a[2] + a[3])
    other = swap(value, "y_hi", 2, 1)
    item_grad = pass2(base, catalog, us, infos, items, SPLIT[0], SPLIT[1], item_grad)
    value = (value + other).astype(bf16)
    got = [value] + [swap(value, "x", 4, k) for k in (1, 2, 3)]
    item_grad = pass2(base, catalog, us, infos, items, SPLIT[1], items, item_grad)
    got = jnp.stack(got)
    user_grad = jnp.concatenate(
        [lax.dynamic_index_in_dim(got, x ^ k, keepdims=False) for k in range(4)], axis=0
    )
    return loss.reshape(rows), user_grad, item_grad


SPLIT = (512, 1024)


def solution(mesh):
    grid = Mesh(mesh.devices.reshape(2, 2, 4, 2, 4), USER + ITEM)

    return jax.shard_map(
        per_device,
        mesh=grid,
        in_specs=(P(USER, None), P(ITEM, None), P(USER)),
        out_specs=(P(USER), P(USER, None), P(ITEM + USER, None)),
        check_vma=False,
    )
```

```python
import functools
import math

import jax
import jax.numpy as jnp
from jax import lax
from jax.experimental import pallas as pl
from jax.experimental.pallas import tpu as pltpu
from jax.sharding import Mesh
from jax.sharding import PartitionSpec as P

sharpness_divisor = 4.0
SCALE = math.log2(math.e) / sharpness_divisor
NT = (((1,), (1,)), ((), ()))
ITEM = ("z", "y_hi", "x")
USER = ("y_lo", "core")
VMEM = pl.BlockSpec(memory_space=pltpu.VMEM)
SMEM = pl.BlockSpec(memory_space=pltpu.SMEM)
ANY = pl.BlockSpec(memory_space=pl.ANY)
f32 = jnp.float32
bf16 = jnp.bfloat16


def exp_of(x):
    return jnp.exp2(x * SCALE)


def struct(*shape, dtype=f32):
    return jax.ShapeDtypeStruct(shape, dtype)


def as_row(column):
    return jnp.broadcast_to(column, (128, 128)).T[0:1]


def as_column(row):
    return jnp.broadcast_to(row, (128, 128)).T


def pass1_kernel(tile, rb, u_ref, cat_ref, *refs):
    out_refs, every_ref, (c_ref, acc_ref, m_ref, l_ref, st_ref, sem) = refs[:4], refs[4], refs[5:]
    rows = u_ref.shape[0]
    count, width = cat_ref.shape
    n = count // tile
    copies = []
    for i in range(n):
        part = pl.ds(i * tile, tile)
        copies.append(pltpu.make_async_copy(cat_ref.at[part], c_ref.at[part], sem.at[i]))
        copies[-1].start()
    acc_ref[...] = jnp.zeros_like(acc_ref)
    m_ref[...] = jnp.full_like(m_ref, -1e38)
    l_ref[...] = jnp.zeros_like(l_ref)
    for i in range(n):
        copies[i].wait()
        c = c_ref[i * tile : (i + 1) * tile]
        for b in range(rows // rb):
            sl = slice(b * rb, (b + 1) * rb)
            r = lax.dot_general(u_ref[sl], c, NT, preferred_element_type=f32)
            m_old = m_ref[sl]
            m_new = jnp.maximum(m_old, jnp.max(r, axis=1, keepdims=True))
            alpha = exp_of(m_old - m_new)
            m_ref[sl] = m_new
            total = l_ref[sl] * alpha
            ps = []
            for j in range(tile // 128):
                p = exp_of(r[:, j * 128 : (j + 1) * 128] - m_new)
                total = total + p
                ps.append(p.astype(bf16))
            l_ref[sl] = total
            wide = jnp.concatenate([alpha] * (width // 128), axis=1)
            acc_ref[sl] = acc_ref[sl] * wide + jnp.dot(
                jnp.concatenate(ps, axis=1), c, preferred_element_type=f32
            )
    for b in range(rows // 128):
        sl = slice(b * 128, (b + 1) * 128)
        total = jnp.sum(l_ref[sl], axis=1, keepdims=True)
        acc_ref[sl] = acc_ref[sl] * (1.0 / total)
        st_ref[b : b + 1] = m_ref[sl].T[0:1] + sharpness_divisor * jnp.log(as_row(total))
    every_ref[...] = jnp.broadcast_to(st_ref[...][None], every_ref.shape)
    x = lax.axis_index("x")
    chunk = rows // 4
    for k, out_ref in enumerate(out_refs):
        part = pl.ds(pl.multiple_of((x ^ k) * chunk, chunk), chunk)
        out_ref[...] = acc_ref[part, :].astype(bf16)


def pass1(users, catalog, tile=2048, rb=256):
    rows, width = users.shape
    count = catalog.shape[0]
    return pl.pallas_call(
        functools.partial(pass1_kernel, tile, rb),
        in_specs=[VMEM, ANY],
        out_specs=[VMEM] * 5,
        out_shape=[struct(rows // 4, width, dtype=bf16)] * 4 + [struct(128, rows // 128, 128)],
        scratch_shapes=[
            pltpu.VMEM((count, width), bf16),
            pltpu.VMEM((rows, width), f32),
            pltpu.VMEM((rows, 128), f32),
            pltpu.VMEM((rows, 128), f32),
            pltpu.VMEM((rows // 128, 128), f32),
            pltpu.SemaphoreType.DMA((count // tile,)),
        ],
        cost_estimate=pl.CostEstimate(
            flops=4 * rows * count * width, bytes_accessed=2 * count * width, transcendentals=rows * count
        ),
        name="pass1",
    )(users, catalog)


def hits_kernel(pos_ref, u_ref, c_ref, *refs):
    out_refs, own_ref, hit_ref, sp_ref = refs[:4], refs[4], refs[5], refs[6]
    rows, width = u_ref.shape
    count = c_ref.shape[0]
    items = own_ref.shape[0]
    x, member, shard = lax.axis_index("x"), lax.axis_index(USER), lax.axis_index(ITEM)
    own_ref[...] = c_ref[pl.ds(pl.multiple_of(member * items, items), items), :]
    hit_ref[...] = jnp.zeros_like(hit_ref)
    base = shard * count

    @pl.loop(0, rows // 8)
    def _(g):
        here = [pos_ref[g * 8 + j] - base for j in range(8)]
        mine = [(h >= 0) & (h < count) for h in here]

        @pl.when(functools.reduce(jnp.logical_or, mine))
        def _():
            for j in range(8):

                @pl.when(mine[j])
                def _():
                    start = pl.multiple_of((here[j] >> 4) << 4, 16)
                    group = c_ref[pl.ds(start, 16), :].astype(f32)
                    inside = lax.broadcasted_iota(jnp.int32, group.shape, 0) == (here[j] & 15)
                    row = jnp.sum(jnp.where(inside, group, 0.0), axis=0, keepdims=True)
                    hit_ref[pl.ds(g * 8 + j, 1), :] = row

    for b in range(rows // 128):
        sl = slice(b * 128, (b + 1) * 128)
        score = jnp.sum(hit_ref[sl] * u_ref[sl].astype(f32), axis=1, keepdims=True)
        sp_ref[b : b + 1] = as_row(score)
    chunk = rows // 4
    for k, out_ref in enumerate(out_refs):
        part = pl.ds(pl.multiple_of((x ^ k) * chunk, chunk), chunk)
        out_ref[0:chunk] = hit_ref[part, :].astype(bf16)
        rest = jnp.concatenate([sp_ref[pl.ds((x ^ k) * 2 + h, 1), :] for h in range(2)], axis=1)
        terms = []
        for _ in range(3):
            term = rest.astype(bf16).astype(f32)
            rest = rest - term
            terms.append(term)
        terms.append(jnp.zeros((13, width), f32))
        out_ref[chunk:] = jnp.concatenate(terms, axis=0).astype(bf16)


def find_hits(positives, users, catalog):
    rows, width = users.shape
    count = catalog.shape[0]
    return pl.pallas_call(
        hits_kernel,
        in_specs=[SMEM, VMEM, VMEM],
        out_specs=[VMEM] * 5,
        out_shape=[struct(rows // 4 + 16, width, dtype=bf16)] * 4 + [struct(count // 4, width, dtype=bf16)],
        scratch_shapes=[pltpu.VMEM((rows, width), f32), pltpu.VMEM((rows // 128, 128), f32)],
        cost_estimate=pl.CostEstimate(
            flops=rows * count * width // 2, bytes_accessed=2 * count * width, transcendentals=0
        ),
        name="hits",
    )(positives, users, catalog)


def combine_kernel(all_ref, *refs):
    u_refs, h_refs, l_refs, out_ref = refs[:4], refs[4:8], refs[8:12], refs[12]
    x, member, shard = lax.axis_index("x"), lax.axis_index(USER), lax.axis_index(ITEM)
    shards = all_ref.shape[0] // 4
    chunk, width = u_refs[0].shape
    for k, l_ref in enumerate(l_refs):
        stats = all_ref[pl.ds((member ^ k) * shards, shards)]
        top = jnp.max(stats, axis=0)
        l_ref[...] = top + sharpness_divisor * jnp.log(jnp.sum(exp_of(stats - top[None]), axis=0))
    for h in range(chunk // 128):
        sl = slice(h * 128, (h + 1) * 128)
        row = pl.ds(x * 2 + h, 1)
        total = jnp.zeros((128, width), f32)
        for k in range(4):
            weight = exp_of(all_ref[member * shards + (shard ^ k), row, :] - l_refs[0][row, :])
            wide = jnp.concatenate([as_column(weight)] * (width // 128), axis=1)
            total = total + wide * u_refs[k][sl].astype(f32) - h_refs[k][sl].astype(f32)
        out_ref[sl] = (total / sharpness_divisor).astype(bf16)
    scores = [h_ref[chunk:].astype(f32) for h_ref in h_refs]
    out_ref[chunk:] = ((scores[0] + scores[1]) + (scores[2] + scores[3])).astype(bf16)


def combine(every, us, hs):
    rows, width = hs[0].shape
    return pl.pallas_call(
        combine_kernel,
        in_specs=[VMEM] * 9,
        out_specs=[VMEM] * 5,
        out_shape=[struct(*every.shape[1:])] * 4 + [struct(rows, width, dtype=bf16)],
        name="combine",
    )(every, *us, *hs)


def finish_kernel(lse_ref, *refs):
    parts, out_ref, loss_ref = refs[:4], refs[4], refs[5]
    x = lax.axis_index("x")
    chunk = out_ref.shape[0] // 4
    for k, part in enumerate(parts):
        out_ref[pl.ds(pl.multiple_of((x ^ k) * chunk, chunk), chunk), :] = part[0:chunk]
        terms = part[chunk:].astype(f32)
        score = terms[0:1] + terms[1:2] + terms[2:3]
        for h in range(2):
            row = pl.ds((x ^ k) * 2 + h, 1)
            loss_ref[row, :] = (lse_ref[row, :] - score[:, h * 128 : (h + 1) * 128]) / sharpness_divisor


def finish(lse4, parts, rows):
    width = parts[0].shape[1]
    return pl.pallas_call(
        finish_kernel,
        in_specs=[VMEM] * 5,
        out_specs=[VMEM] * 2,
        out_shape=[struct(rows, width, dtype=bf16), struct(*lse4.shape)],
        name="finish",
    )(lse4, *parts)


def pass2_kernel(tile, lead, c_ref, *refs):
    us, lses, poss, out_ref = refs[:4], refs[4:8], refs[8:12], refs[-1]
    member, shard = lax.axis_index(USER), lax.axis_index(ITEM)
    start = (lead + pl.program_id(0)) * tile
    items = c_ref.shape[0]
    c = c_ref[pl.ds(pl.multiple_of(start, tile), tile), :]
    item = lax.broadcasted_iota(jnp.int32, (tile, 128), 0) + (shard * 4 + member) * items + start
    total = jnp.zeros((tile, c.shape[1]), f32)
    for u_ref, l_ref, pos_ref in zip(us, lses, poss):
        u = u_ref[...]
        r = lax.dot_general(c, u, NT, preferred_element_type=f32)
        ws = []
        for j in range(u.shape[0] // 128):
            w = exp_of(r[:, j * 128 : (j + 1) * 128] - l_ref[j : j + 1])
            ws.append(jnp.where(pos_ref[j : j + 1] == item, w - 1.0, w).astype(bf16))
        total = total + jnp.dot(jnp.concatenate(ws, axis=1), u, preferred_element_type=f32)
    out_ref[...] = (total / sharpness_divisor).astype(out_ref.dtype)


def pass2(own, us, lses, poss, start, stop, before, tile=512):
    items, width = own.shape
    rows = us[0].shape[0]
    lead = start // tile
    in_specs = [VMEM] * 13
    args = [own, *us, *lses, *poss]
    aliases = {}
    if before is not None:
        in_specs.append(ANY)
        aliases = {len(args): 0}
        args.append(before)
    return pl.pallas_call(
        functools.partial(pass2_kernel, tile, lead),
        grid=((stop - start) // tile,),
        in_specs=in_specs,
        out_specs=pl.BlockSpec((tile, width), lambda i: (lead + i, 0)),
        out_shape=struct(items, width, dtype=bf16),
        input_output_aliases=aliases,
        cost_estimate=pl.CostEstimate(
            flops=16 * rows * (stop - start) * width,
            bytes_accessed=8 * rows * width,
            transcendentals=4 * rows * (stop - start),
        ),
        name="pass2",
    )(*args)


def swap(x, axis, size, k):
    return lax.ppermute(x, axis, [(i, i ^ k) for i in range(size)])


def per_device(users, catalog, positives):
    rows = users.shape[0]
    items = catalog.shape[0] // 4
    pos = positives.reshape(rows // 128, 128)
    over = swap(users, USER, 4, 2)
    us = [users, swap(users, USER, 4, 1), over, swap(over, USER, 4, 1)]
    poss = [pos] + [swap(pos, USER, 4, k) for k in (1, 2, 3)]
    *pieces, every = pass1(users, catalog)
    every = lax.all_to_all(every, USER + ITEM, 0, 0, tiled=True)
    *hits, own = find_hits(positives, users, catalog)
    pieces = [pieces[0]] + [swap(pieces[k], "x", 4, k) for k in (1, 2, 3)]
    hits = [hits[0]] + [swap(hits[k], "x", 4, k) for k in (1, 2, 3)]
    *lses, value = combine(every, pieces, hits)

    a = [value] + [swap(value, "z", 4, k) for k in (1, 2, 3)]
    item_grad = pass2(own, us, lses, poss, 0, SPLIT[0], None)
    a = [v.astype(f32) for v in a]
    value = (a[0] + a[1]) + (a[2] + a[3])
    other = swap(value, "y_hi", 2, 1)
    item_grad = pass2(own, us, lses, poss, SPLIT[0], SPLIT[1], item_grad)
    value = (value + other).astype(bf16)
    got = [value] + [swap(value, "x", 4, k) for k in (1, 2, 3)]
    item_grad = pass2(own, us, lses, poss, SPLIT[1], items, item_grad)
    user_grad, loss = finish(lses[0], got, rows)
    return loss.reshape(rows), user_grad, item_grad


SPLIT = (512, 1024)


def solution(mesh):
    grid = Mesh(mesh.devices.reshape(2, 2, 4, 2, 4), USER + ITEM)

    return jax.shard_map(
        per_device,
        mesh=grid,
        in_specs=(P(USER, None), P(ITEM, None), P(USER)),
        out_specs=(P(USER), P(USER, None), P(ITEM + USER, None)),
        check_vma=False,
    )
```

```python
import functools
import math

import jax
import jax.numpy as jnp
from jax import lax
from jax.experimental import pallas as pl
from jax.experimental.pallas import tpu as pltpu
from jax.sharding import Mesh
from jax.sharding import PartitionSpec as P

sharpness_divisor = 4.0
SCALE = math.log2(math.e) / sharpness_divisor
NT = (((1,), (1,)), ((), ()))
ITEM = ("z", "y_hi", "x")
USER = ("y_lo", "core")
VMEM = pl.BlockSpec(memory_space=pltpu.VMEM)
SMEM = pl.BlockSpec(memory_space=pltpu.SMEM)
ANY = pl.BlockSpec(memory_space=pl.ANY)
HBM = pl.BlockSpec(memory_space=pltpu.HBM)
f32 = jnp.float32
bf16 = jnp.bfloat16
MIB = 1 << 20


def exp_of(x):
    return jnp.exp2(x * SCALE)


def near(xs):
    return [pltpu.with_memory_space_constraint(x, pltpu.VMEM) for x in xs]


def far(x):
    return pltpu.with_memory_space_constraint(x, pltpu.HBM)


def struct(*shape, dtype=f32):
    return jax.ShapeDtypeStruct(shape, dtype)


def as_row(column):
    return jnp.broadcast_to(column, (128, 128)).T[0:1]


def as_column(row):
    return jnp.broadcast_to(row, (128, 128)).T


def pass1_kernel(tile, rb, u_ref, pos_ref, cat_ref, *refs):
    out_refs, every_ref, (c_ref, acc_ref, m_ref, l_ref, st_ref, sem) = refs[:4], refs[4], refs[5:]
    rows = u_ref.shape[0]
    count, width = cat_ref.shape
    n = count // tile
    copies = []
    for i in range(n):
        part = pl.ds(i * tile, tile)
        copies.append(pltpu.make_async_copy(cat_ref.at[part], c_ref.at[part], sem.at[i]))
        copies[-1].start()
    acc_ref[...] = jnp.zeros_like(acc_ref)
    m_ref[...] = jnp.full_like(m_ref, -1e38)
    l_ref[...] = jnp.zeros_like(l_ref)
    for i in range(n):
        copies[i].wait()
        c = c_ref[i * tile : (i + 1) * tile]
        for b in range(rows // rb):
            sl = slice(b * rb, (b + 1) * rb)
            r = lax.dot_general(u_ref[sl], c, NT, preferred_element_type=f32)
            m_old = m_ref[sl]
            m_new = jnp.maximum(m_old, jnp.max(r, axis=1, keepdims=True))
            alpha = exp_of(m_old - m_new)
            m_ref[sl] = m_new
            total = l_ref[sl] * alpha
            ps = []
            for j in range(tile // 128):
                p = exp_of(r[:, j * 128 : (j + 1) * 128] - m_new)
                total = total + p
                ps.append(p.astype(bf16))
            l_ref[sl] = total
            wide = jnp.concatenate([alpha] * (width // 128), axis=1)
            acc_ref[sl] = acc_ref[sl] * wide + jnp.dot(
                jnp.concatenate(ps, axis=1), c, preferred_element_type=f32
            )
    for b in range(rows // 128):
        sl = slice(b * 128, (b + 1) * 128)
        total = jnp.sum(l_ref[sl], axis=1, keepdims=True)
        acc_ref[sl] = acc_ref[sl] * (1.0 / total)
        st_ref[b : b + 1] = m_ref[sl].T[0:1] + sharpness_divisor * jnp.log(as_row(total))
    st_ref[rows // 128 :] = pos_ref[...].astype(f32)
    every_ref[...] = jnp.broadcast_to(st_ref[...][None], every_ref.shape)
    x = lax.axis_index("x")
    chunk = rows // 4
    for k, out_ref in enumerate(out_refs):
        part = pl.ds(pl.multiple_of((x ^ k) * chunk, chunk), chunk)
        out_ref[...] = acc_ref[part, :].astype(bf16)


def pass1(users, pos, catalog, tile=2048, rb=256):
    rows, width = users.shape
    count = catalog.shape[0]
    return pl.pallas_call(
        functools.partial(pass1_kernel, tile, rb),
        in_specs=[VMEM, VMEM, HBM],
        out_specs=[VMEM] * 5,
        out_shape=[struct(rows // 4, width, dtype=bf16)] * 4 + [struct(128, rows // 64, 128)],
        scratch_shapes=[
            pltpu.VMEM((count, width), bf16),
            pltpu.VMEM((rows, width), f32),
            pltpu.VMEM((rows, 128), f32),
            pltpu.VMEM((rows, 128), f32),
            pltpu.VMEM((rows // 64, 128), f32),
            pltpu.SemaphoreType.DMA((count // tile,)),
        ],
        cost_estimate=pl.CostEstimate(
            flops=4 * rows * count * width, bytes_accessed=2 * count * width, transcendentals=rows * count
        ),
        compiler_params=pltpu.CompilerParams(vmem_limit_bytes=20 * MIB),
        name="pass1",
    )(users, pos, far(catalog))


def hits_kernel(pos_ref, u_ref, cat_ref, *refs):
    out_refs, own_ref, (hit_ref, sp_ref, c_ref, found_ref, sem) = refs[:4], refs[4], refs[5:]
    rows, width = u_ref.shape
    count = cat_ref.shape[0]
    items = own_ref.shape[0]
    x, member, shard = lax.axis_index("x"), lax.axis_index(USER), lax.axis_index(ITEM)
    mine = pl.ds(pl.multiple_of(member * items, items), items)
    whole_copy = pltpu.make_async_copy(cat_ref, c_ref, sem.at[0])
    own_copy = pltpu.make_async_copy(cat_ref.at[mine], own_ref, sem.at[1])
    whole_copy.start()
    own_copy.start()
    hit_ref[...] = jnp.zeros_like(hit_ref)
    base = shard * count
    bits = count.bit_length() - 1

    def scan(g, n):
        for j in range(16):
            found_ref[n] = g * 16 + j
            n = n + ((pos_ref[g * 16 + j] >> bits) == shard).astype(jnp.int32)
        return n

    n_found = lax.fori_loop(0, rows // 16, scan, jnp.int32(0))
    whole_copy.wait()

    @pl.loop(0, n_found)
    def _(i):
        user = found_ref[i]
        here = pos_ref[user] - base
        group = c_ref[pl.ds(pl.multiple_of((here >> 4) << 4, 16), 16), :].astype(f32)
        inside = lax.broadcasted_iota(jnp.int32, group.shape, 0) == (here & 15)
        hit_ref[pl.ds(user, 1), :] = jnp.sum(jnp.where(inside, group, 0.0), axis=0, keepdims=True)

    for b in range(rows // 128):
        sl = slice(b * 128, (b + 1) * 128)
        score = jnp.sum(hit_ref[sl] * u_ref[sl].astype(f32), axis=1, keepdims=True)
        sp_ref[b : b + 1] = as_row(score)
    chunk = rows // 4
    for k, out_ref in enumerate(out_refs):
        part = pl.ds(pl.multiple_of((x ^ k) * chunk, chunk), chunk)
        out_ref[0:chunk] = hit_ref[part, :].astype(bf16)
        rest = jnp.concatenate([sp_ref[pl.ds((x ^ k) * 2 + h, 1), :] for h in range(2)], axis=1)
        terms = []
        for _ in range(3):
            term = rest.astype(bf16).astype(f32)
            rest = rest - term
            terms.append(term)
        terms.append(jnp.zeros((13, width), f32))
        out_ref[chunk:] = jnp.concatenate(terms, axis=0).astype(bf16)
    own_copy.wait()


def find_hits(positives, users, catalog):
    rows, width = users.shape
    count = catalog.shape[0]
    return pl.pallas_call(
        hits_kernel,
        in_specs=[SMEM, VMEM, HBM],
        out_specs=[VMEM] * 5,
        out_shape=[struct(rows // 4 + 16, width, dtype=bf16)] * 4 + [struct(count // 4, width, dtype=bf16)],
        scratch_shapes=[
            pltpu.VMEM((rows, width), f32),
            pltpu.VMEM((rows // 128, 128), f32),
            pltpu.VMEM((count, width), bf16),
            pltpu.SMEM((rows,), jnp.int32),
            pltpu.SemaphoreType.DMA((2,)),
        ],
        cost_estimate=pl.CostEstimate(
            flops=rows * count * width // 2, bytes_accessed=2 * count * width, transcendentals=0
        ),
        compiler_params=pltpu.CompilerParams(vmem_limit_bytes=12 * MIB),
        name="hits",
    )(positives, users, far(catalog))


def combine_kernel(all_ref, *refs):
    u_refs, h_refs, l_refs, out_ref = refs[:4], refs[4:8], refs[8:12], refs[12]
    x, member, shard = lax.axis_index("x"), lax.axis_index(USER), lax.axis_index(ITEM)
    shards = all_ref.shape[0] // 4
    chunk, width = u_refs[0].shape
    half = all_ref.shape[1] // 2
    for k, l_ref in enumerate(l_refs):
        first = (member ^ k) * shards
        stats = all_ref[pl.ds(first, shards), 0:half]
        top = jnp.max(stats, axis=0)
        l_ref[0:half] = top + sharpness_divisor * jnp.log(jnp.sum(exp_of(stats - top[None]), axis=0))
        l_ref[half:] = all_ref[first, half:]
    for h in range(chunk // 128):
        sl = slice(h * 128, (h + 1) * 128)
        row = pl.ds(x * 2 + h, 1)
        total = jnp.zeros((128, width), f32)
        for k in range(4):
            weight = exp_of(all_ref[member * shards + (shard ^ k), row, :] - l_refs[0][row, :])
            wide = jnp.concatenate([as_column(weight)] * (width // 128), axis=1)
            total = total + wide * u_refs[k][sl].astype(f32) - h_refs[k][sl].astype(f32)
        out_ref[sl] = (total / sharpness_divisor).astype(bf16)
    scores = [h_ref[chunk:].astype(f32) for h_ref in h_refs]
    out_ref[chunk:] = ((scores[0] + scores[1]) + (scores[2] + scores[3])).astype(bf16)


def combine(every, us, hs):
    rows, width = hs[0].shape
    return pl.pallas_call(
        combine_kernel,
        in_specs=[VMEM] * 9,
        out_specs=[VMEM] * 5,
        out_shape=[struct(*every.shape[1:])] * 4 + [struct(rows, width, dtype=bf16)],
        compiler_params=pltpu.CompilerParams(vmem_limit_bytes=8 * MIB),
        name="combine",
    )(*near([every, *us, *hs]))


def finish_kernel(lse_ref, *refs):
    parts, out_ref, loss_ref = refs[:4], refs[4], refs[5]
    x = lax.axis_index("x")
    chunk = out_ref.shape[0] // 4
    for k, part in enumerate(parts):
        out_ref[pl.ds(pl.multiple_of((x ^ k) * chunk, chunk), chunk), :] = part[0:chunk]
        terms = part[chunk:].astype(f32)
        score = terms[0:1] + terms[1:2] + terms[2:3]
        for h in range(2):
            row = pl.ds((x ^ k) * 2 + h, 1)
            loss_ref[row, :] = (lse_ref[row, :] - score[:, h * 128 : (h + 1) * 128]) / sharpness_divisor


def finish(lse4, parts, rows):
    width = parts[0].shape[1]
    return pl.pallas_call(
        finish_kernel,
        in_specs=[VMEM] * 5,
        out_specs=[VMEM] * 2,
        out_shape=[struct(rows, width, dtype=bf16), struct(rows // 128, 128)],
        compiler_params=pltpu.CompilerParams(vmem_limit_bytes=6 * MIB),
        name="finish",
    )(*near([lse4, *parts]))


def pass2_kernel(tile, lead, c_ref, *refs):
    us, infos, out_ref = refs[:4], refs[4:8], refs[-1]
    member, shard = lax.axis_index(USER), lax.axis_index(ITEM)
    start = (lead + pl.program_id(0)) * tile
    items = c_ref.shape[0]
    c = c_ref[pl.ds(pl.multiple_of(start, tile), tile), :]
    item = lax.broadcasted_iota(jnp.int32, (tile, 128), 0) + (shard * 4 + member) * items + start
    item = item.astype(f32)
    total = jnp.zeros((tile, c.shape[1]), f32)
    for u_ref, info_ref in zip(us, infos):
        u = u_ref[...]
        blocks = u.shape[0] // 128
        r = lax.dot_general(c, u, NT, preferred_element_type=f32)
        ws = []
        for j in range(blocks):
            w = exp_of(r[:, j * 128 : (j + 1) * 128] - info_ref[j : j + 1])
            hit = info_ref[blocks + j : blocks + j + 1] == item
            ws.append(jnp.where(hit, w - 1.0, w).astype(bf16))
        total = total + jnp.dot(jnp.concatenate(ws, axis=1), u, preferred_element_type=f32)
    out_ref[...] = (total / sharpness_divisor).astype(out_ref.dtype)


def pass2(own, us, infos, start, stop, before, tile=512):
    items, width = own.shape
    rows = us[0].shape[0]
    lead = start // tile
    in_specs = [VMEM] * 9
    args = [own, *us, *infos]
    aliases = {}
    if before is not None:
        in_specs.append(ANY)
        aliases = {len(args): 0}
        args.append(before)
    return pl.pallas_call(
        functools.partial(pass2_kernel, tile, lead),
        grid=((stop - start) // tile,),
        in_specs=in_specs,
        out_specs=pl.BlockSpec((tile, width), lambda i: (lead + i, 0)),
        out_shape=struct(items, width, dtype=bf16),
        input_output_aliases=aliases,
        cost_estimate=pl.CostEstimate(
            flops=16 * rows * (stop - start) * width,
            bytes_accessed=8 * rows * width,
            transcendentals=4 * rows * (stop - start),
        ),
        compiler_params=pltpu.CompilerParams(vmem_limit_bytes=14 * MIB),
        name="pass2",
    )(*near(args[:9]), *args[9:])


def swap(x, axis, size, k):
    return lax.ppermute(x, axis, [(i, i ^ k) for i in range(size)])


def per_device(users, catalog, positives):
    rows = users.shape[0]
    items = catalog.shape[0] // 4
    pos = positives.reshape(rows // 128, 128)
    over = swap(users, USER, 4, 2)
    us = [users, swap(users, USER, 4, 1), over, swap(over, USER, 4, 1)]
    *pieces, every = pass1(users, pos, catalog)
    every = lax.all_to_all(every, USER + ITEM, 0, 0, tiled=True)
    *hits, own = find_hits(positives, users, catalog)
    pieces = [pieces[0]] + [swap(pieces[k], "x", 4, k) for k in (1, 2, 3)]
    hits = [hits[0]] + [swap(hits[k], "x", 4, k) for k in (1, 2, 3)]
    *infos, value = combine(every, pieces, hits)

    a = [value] + [swap(value, "z", 4, k) for k in (1, 2, 3)]
    item_grad = pass2(own, us, infos, 0, SPLIT[0], None)
    a = [v.astype(f32) for v in a]
    value = (a[0] + a[1]) + (a[2] + a[3])
    other = swap(value, "y_hi", 2, 1)
    item_grad = pass2(own, us, infos, SPLIT[0], SPLIT[1], item_grad)
    value = (value + other).astype(bf16)
    got = [value] + [swap(value, "x", 4, k) for k in (1, 2, 3)]
    item_grad = pass2(own, us, infos, SPLIT[1], items, item_grad)
    user_grad, loss = finish(infos[0], got, rows)
    return loss.reshape(rows), user_grad, item_grad


SPLIT = (512, 1024)


def solution(mesh):
    grid = Mesh(mesh.devices.reshape(2, 2, 4, 2, 4), USER + ITEM)

    return jax.shard_map(
        per_device,
        mesh=grid,
        in_specs=(P(USER, None), P(ITEM, None), P(USER)),
        out_specs=(P(USER), P(USER, None), P(ITEM + USER, None)),
        check_vma=False,
    )
```

```python
import functools
import math

import jax
import jax.numpy as jnp
from jax import lax
from jax.experimental import pallas as pl
from jax.experimental.pallas import tpu as pltpu
from jax.sharding import Mesh
from jax.sharding import PartitionSpec as P

sharpness_divisor = 4.0
SCALE = math.log2(math.e) / sharpness_divisor
NT = (((1,), (1,)), ((), ()))
ITEM = ("z", "y_hi", "x")
USER = ("y_lo", "core")
VMEM = pl.BlockSpec(memory_space=pltpu.VMEM)
SMEM = pl.BlockSpec(memory_space=pltpu.SMEM)
ANY = pl.BlockSpec(memory_space=pl.ANY)
HBM = pl.BlockSpec(memory_space=pltpu.HBM)
f32 = jnp.float32
bf16 = jnp.bfloat16
MIB = 1 << 20


def exp_of(x):
    return jnp.exp2(x * SCALE)


def near(xs):
    return [pltpu.with_memory_space_constraint(x, pltpu.VMEM) for x in xs]


def far(x):
    return pltpu.with_memory_space_constraint(x, pltpu.HBM)


def struct(*shape, dtype=f32):
    return jax.ShapeDtypeStruct(shape, dtype)


def as_row(column):
    return jnp.broadcast_to(column, (128, 128)).T[0:1]


def as_column(row):
    return jnp.broadcast_to(row, (128, 128)).T


def pass1_kernel(tile, rb, u_ref, cat_ref, *refs):
    out_refs, every_ref, (c_ref, acc_ref, m_ref, l_ref, st_ref, sem) = refs[:4], refs[4], refs[5:]
    rows = u_ref.shape[0]
    count, width = cat_ref.shape
    n = count // tile
    copies = []
    for i in range(n):
        part = pl.ds(i * tile, tile)
        copies.append(pltpu.make_async_copy(cat_ref.at[part], c_ref.at[part], sem.at[i]))
        copies[-1].start()
    acc_ref[...] = jnp.zeros_like(acc_ref)
    m_ref[...] = jnp.full_like(m_ref, -1e38)
    l_ref[...] = jnp.zeros_like(l_ref)
    for i in range(n):
        copies[i].wait()
        c = c_ref[i * tile : (i + 1) * tile]
        for b in range(rows // rb):
            sl = slice(b * rb, (b + 1) * rb)
            r = lax.dot_general(u_ref[sl], c, NT, preferred_element_type=f32)
            m_old = m_ref[sl]
            m_new = jnp.maximum(m_old, jnp.max(r, axis=1, keepdims=True))
            alpha = exp_of(m_old - m_new)
            m_ref[sl] = m_new
            total = l_ref[sl] * alpha
            ps = []
            for j in range(tile // 128):
                p = exp_of(r[:, j * 128 : (j + 1) * 128] - m_new)
                total = total + p
                ps.append(p.astype(bf16))
            l_ref[sl] = total
            wide = jnp.concatenate([alpha] * (width // 128), axis=1)
            acc_ref[sl] = acc_ref[sl] * wide + jnp.dot(
                jnp.concatenate(ps, axis=1), c, preferred_element_type=f32
            )
    for b in range(rows // 128):
        sl = slice(b * 128, (b + 1) * 128)
        total = jnp.sum(l_ref[sl], axis=1, keepdims=True)
        acc_ref[sl] = acc_ref[sl] * (1.0 / total)
        st_ref[b : b + 1] = m_ref[sl].T[0:1] + sharpness_divisor * jnp.log(as_row(total))
    every_ref[...] = jnp.broadcast_to(st_ref[...][None], every_ref.shape)
    x = lax.axis_index("x")
    chunk = rows // 4
    for k, out_ref in enumerate(out_refs):
        part = pl.ds(pl.multiple_of((x ^ k) * chunk, chunk), chunk)
        out_ref[...] = acc_ref[part, :].astype(bf16)


def pass1(users, catalog, tile=2048, rb=256):
    rows, width = users.shape
    count = catalog.shape[0]
    return pl.pallas_call(
        functools.partial(pass1_kernel, tile, rb),
        in_specs=[VMEM, HBM],
        out_specs=[VMEM] * 5,
        out_shape=[struct(rows // 4, width, dtype=bf16)] * 4 + [struct(128, rows // 128, 128)],
        scratch_shapes=[
            pltpu.VMEM((count, width), bf16),
            pltpu.VMEM((rows, width), f32),
            pltpu.VMEM((rows, 128), f32),
            pltpu.VMEM((rows, 128), f32),
            pltpu.VMEM((rows // 128, 128), f32),
            pltpu.SemaphoreType.DMA((count // tile,)),
        ],
        cost_estimate=pl.CostEstimate(
            flops=4 * rows * count * width, bytes_accessed=2 * count * width, transcendentals=rows * count
        ),
        compiler_params=pltpu.CompilerParams(vmem_limit_bytes=20 * MIB),
        name="pass1",
    )(users, far(catalog))


def hits_kernel(pos_ref, u_ref, cat_ref, *refs):
    out_refs, (hit_ref, sp_ref, c_ref, found_ref, sem) = refs[:4], refs[4:]
    rows, width = u_ref.shape
    count = cat_ref.shape[0]
    x, shard = lax.axis_index("x"), lax.axis_index(ITEM)
    whole_copy = pltpu.make_async_copy(cat_ref, c_ref, sem)
    whole_copy.start()
    hit_ref[...] = jnp.zeros_like(hit_ref)
    base = shard * count
    bits = count.bit_length() - 1

    def scan(g, n):
        for j in range(16):
            found_ref[n] = g * 16 + j
            n = n + ((pos_ref[g * 16 + j] >> bits) == shard).astype(jnp.int32)
        return n

    n_found = lax.fori_loop(0, rows // 16, scan, jnp.int32(0))
    whole_copy.wait()

    @pl.loop(0, n_found)
    def _(i):
        user = found_ref[i]
        here = pos_ref[user] - base
        group = c_ref[pl.ds(pl.multiple_of((here >> 4) << 4, 16), 16), :].astype(f32)
        inside = lax.broadcasted_iota(jnp.int32, group.shape, 0) == (here & 15)
        hit_ref[pl.ds(user, 1), :] = jnp.sum(jnp.where(inside, group, 0.0), axis=0, keepdims=True)

    for b in range(rows // 128):
        sl = slice(b * 128, (b + 1) * 128)
        score = jnp.sum(hit_ref[sl] * u_ref[sl].astype(f32), axis=1, keepdims=True)
        sp_ref[b : b + 1] = as_row(score)
    chunk = rows // 4
    for k, out_ref in enumerate(out_refs):
        part = pl.ds(pl.multiple_of((x ^ k) * chunk, chunk), chunk)
        out_ref[0:chunk] = hit_ref[part, :].astype(bf16)
        rest = jnp.concatenate([sp_ref[pl.ds((x ^ k) * 2 + h, 1), :] for h in range(2)], axis=1)
        terms = []
        for _ in range(3):
            term = rest.astype(bf16).astype(f32)
            rest = rest - term
            terms.append(term)
        terms.append(jnp.zeros((13, width), f32))
        out_ref[chunk:] = jnp.concatenate(terms, axis=0).astype(bf16)


def find_hits(positives, users, catalog):
    rows, width = users.shape
    count = catalog.shape[0]
    return pl.pallas_call(
        hits_kernel,
        in_specs=[SMEM, VMEM, HBM],
        out_specs=[VMEM] * 4,
        out_shape=[struct(rows // 4 + 16, width, dtype=bf16)] * 4,
        scratch_shapes=[
            pltpu.VMEM((rows, width), f32),
            pltpu.VMEM((rows // 128, 128), f32),
            pltpu.VMEM((count, width), bf16),
            pltpu.SMEM((rows,), jnp.int32),
            pltpu.SemaphoreType.DMA(()),
        ],
        cost_estimate=pl.CostEstimate(
            flops=rows * count * width // 2, bytes_accessed=2 * count * width, transcendentals=0
        ),
        compiler_params=pltpu.CompilerParams(vmem_limit_bytes=12 * MIB),
        name="hits",
    )(positives, users, far(catalog))


def combine_kernel(all_ref, *refs):
    u_refs, h_refs, l_refs, out_ref = refs[:4], refs[4:8], refs[8:12], refs[12]
    x, member, shard = lax.axis_index("x"), lax.axis_index(USER), lax.axis_index(ITEM)
    shards = all_ref.shape[0] // 4
    chunk, width = u_refs[0].shape
    for k, l_ref in enumerate(l_refs):
        stats = all_ref[pl.ds((member ^ k) * shards, shards)]
        top = jnp.max(stats, axis=0)
        l_ref[...] = top + sharpness_divisor * jnp.log(jnp.sum(exp_of(stats - top[None]), axis=0))
    for h in range(chunk // 128):
        sl = slice(h * 128, (h + 1) * 128)
        row = pl.ds(x * 2 + h, 1)
        total = jnp.zeros((128, width), f32)
        for k in range(4):
            weight = exp_of(all_ref[member * shards + (shard ^ k), row, :] - l_refs[0][row, :])
            wide = jnp.concatenate([as_column(weight)] * (width // 128), axis=1)
            total = total + wide * u_refs[k][sl].astype(f32) - h_refs[k][sl].astype(f32)
        out_ref[sl] = (total / sharpness_divisor).astype(bf16)
    scores = [h_ref[chunk:].astype(f32) for h_ref in h_refs]
    out_ref[chunk:] = ((scores[0] + scores[1]) + (scores[2] + scores[3])).astype(bf16)


def combine(every, us, hs):
    rows, width = hs[0].shape
    return pl.pallas_call(
        combine_kernel,
        in_specs=[VMEM] * 9,
        out_specs=[VMEM] * 5,
        out_shape=[struct(*every.shape[1:])] * 4 + [struct(rows, width, dtype=bf16)],
        compiler_params=pltpu.CompilerParams(vmem_limit_bytes=8 * MIB),
        name="combine",
    )(*near([every, *us, *hs]))


def finish_kernel(lse_ref, *refs):
    parts, out_ref, loss_ref = refs[:4], refs[4], refs[5]
    x = lax.axis_index("x")
    chunk = out_ref.shape[0] // 4
    for k, part in enumerate(parts):
        out_ref[pl.ds(pl.multiple_of((x ^ k) * chunk, chunk), chunk), :] = part[0:chunk]
        terms = part[chunk:].astype(f32)
        score = terms[0:1] + terms[1:2] + terms[2:3]
        for h in range(2):
            row = pl.ds((x ^ k) * 2 + h, 1)
            loss_ref[row, :] = (lse_ref[row, :] - score[:, h * 128 : (h + 1) * 128]) / sharpness_divisor


def finish(lse4, parts, rows):
    width = parts[0].shape[1]
    return pl.pallas_call(
        finish_kernel,
        in_specs=[VMEM] * 5,
        out_specs=[VMEM] * 2,
        out_shape=[struct(rows, width, dtype=bf16), struct(rows // 128, 128)],
        compiler_params=pltpu.CompilerParams(vmem_limit_bytes=6 * MIB),
        name="finish",
    )(*near([lse4, *parts]))


def pass2_kernel(tile, items, lead, c_ref, *refs):
    us, infos, poss, out_ref = refs[:4], refs[4:8], refs[8:12], refs[-1]
    member, shard = lax.axis_index(USER), lax.axis_index(ITEM)
    start = (lead + pl.program_id(0)) * tile
    c = c_ref[...]
    item = lax.broadcasted_iota(jnp.int32, (tile, 128), 0) + (shard * 4 + member) * items + start
    total = jnp.zeros((tile, c.shape[1]), f32)
    for u_ref, info_ref, pos_ref in zip(us, infos, poss):
        u = u_ref[...]
        blocks = u.shape[0] // 128
        r = lax.dot_general(c, u, NT, preferred_element_type=f32)
        ws = []
        for j in range(blocks):
            w = exp_of(r[:, j * 128 : (j + 1) * 128] - info_ref[j : j + 1])
            ws.append(jnp.where(pos_ref[j : j + 1] == item, w - 1.0, w).astype(bf16))
        total = total + jnp.dot(jnp.concatenate(ws, axis=1), u, preferred_element_type=f32)
    out_ref[...] = (total / sharpness_divisor).astype(out_ref.dtype)


def pass2(catalog, us, infos, poss, start, stop, before, tile=512):
    items, width = catalog.shape[0] // 4, catalog.shape[1]
    rows = us[0].shape[0]
    lead = start // tile
    mine = lambda i: (lax.axis_index(USER) * (items // tile) + lead + i, 0)
    in_specs = [pl.BlockSpec((tile, width), mine)] + [VMEM] * 12
    args = [far(catalog), *near([*us, *infos, *poss])]
    aliases = {}
    if before is not None:
        in_specs.append(ANY)
        aliases = {len(args): 0}
        args.append(before)
    return pl.pallas_call(
        functools.partial(pass2_kernel, tile, items, lead),
        grid=((stop - start) // tile,),
        in_specs=in_specs,
        out_specs=pl.BlockSpec((tile, width), lambda i: (lead + i, 0)),
        out_shape=struct(items, width, dtype=bf16),
        input_output_aliases=aliases,
        cost_estimate=pl.CostEstimate(
            flops=16 * rows * (stop - start) * width,
            bytes_accessed=8 * rows * width,
            transcendentals=4 * rows * (stop - start),
        ),
        compiler_params=pltpu.CompilerParams(vmem_limit_bytes=14 * MIB),
        name="pass2",
    )(*args)


def swap(x, axis, size, k):
    return lax.ppermute(x, axis, [(i, i ^ k) for i in range(size)])


def per_device(users, catalog, positives):
    rows = users.shape[0]
    items = catalog.shape[0] // 4
    pos = positives.reshape(rows // 128, 128)
    over = swap(users, USER, 4, 2)
    us = [users, swap(users, USER, 4, 1), over, swap(over, USER, 4, 1)]
    poss = [pos] + [swap(pos, USER, 4, k) for k in (1, 2, 3)]
    *pieces, every = pass1(users, catalog)
    every = lax.all_to_all(every, USER + ITEM, 0, 0, tiled=True)
    hits = find_hits(positives, users, catalog)
    pieces = [pieces[0]] + [swap(pieces[k], "x", 4, k) for k in (1, 2, 3)]
    hits = [hits[0]] + [swap(hits[k], "x", 4, k) for k in (1, 2, 3)]
    *infos, value = combine(every, pieces, hits)

    a = [value] + [swap(value, "z", 4, k) for k in (1, 2, 3)]
    item_grad = pass2(catalog, us, infos, poss, 0, SPLIT[0], None)
    a = [v.astype(f32) for v in a]
    value = (a[0] + a[1]) + (a[2] + a[3])
    other = swap(value, "y_hi", 2, 1)
    item_grad = pass2(catalog, us, infos, poss, SPLIT[0], SPLIT[1], item_grad)
    value = (value + other).astype(bf16)
    got = [value] + [swap(value, "x", 4, k) for k in (1, 2, 3)]
    item_grad = pass2(catalog, us, infos, poss, SPLIT[1], items, item_grad)
    user_grad, loss = finish(infos[0], got, rows)
    return loss.reshape(rows), user_grad, item_grad


SPLIT = (512, 1024)


def solution(mesh):
    grid = Mesh(mesh.devices.reshape(2, 2, 4, 2, 4), USER + ITEM)

    return jax.shard_map(
        per_device,
        mesh=grid,
        in_specs=(P(USER, None), P(ITEM, None), P(USER)),
        out_specs=(P(USER), P(USER, None), P(ITEM + USER, None)),
        check_vma=False,
    )
```

```python
import functools
import math

import jax
import jax.numpy as jnp
from jax import lax
from jax.experimental import pallas as pl
from jax.experimental.pallas import tpu as pltpu
from jax.sharding import Mesh
from jax.sharding import PartitionSpec as P

sharpness_divisor = 4.0
SCALE = math.log2(math.e) / sharpness_divisor
NT = (((1,), (1,)), ((), ()))
ITEM = ("z", "y_hi", "x")
USER = ("y_lo", "core")
VMEM = pl.BlockSpec(memory_space=pltpu.VMEM)
SMEM = pl.BlockSpec(memory_space=pltpu.SMEM)
ANY = pl.BlockSpec(memory_space=pl.ANY)
HBM = pl.BlockSpec(memory_space=pltpu.HBM)
f32 = jnp.float32
bf16 = jnp.bfloat16
MIB = 1 << 20


NEAR = (0, 1, 8, 9)
REST = (0, 3, 24, 27)
ACROSS = 4


def chunk_id():
    x, z = lax.axis_index("x"), lax.axis_index("z")
    return ((x ^ (x >> 1)) & 1) + 2 * ((z ^ (z >> 1)) & 1)


def exp_of(x):
    return jnp.exp2(x * SCALE)


def near(xs):
    return [pltpu.with_memory_space_constraint(x, pltpu.VMEM) for x in xs]


def far(x):
    return pltpu.with_memory_space_constraint(x, pltpu.HBM)


def struct(*shape, dtype=f32):
    return jax.ShapeDtypeStruct(shape, dtype)


def as_row(column):
    return jnp.broadcast_to(column, (128, 128)).T[0:1]


def as_column(row):
    return jnp.broadcast_to(row, (128, 128)).T


def pass1_kernel(tile, rb, users_ref, cat_ref, *refs):
    out_refs, every_ref, (u_ref, c_ref, acc_ref, m_ref, l_ref, st_ref, sem, u_sem) = refs[:4], refs[4], refs[5:]
    rows = u_ref.shape[0]
    u_copy = pltpu.make_async_copy(users_ref, u_ref, u_sem)
    u_copy.start()
    count, width = cat_ref.shape
    n = count // tile
    copies = []
    for i in range(n):
        part = pl.ds(i * tile, tile)
        copies.append(pltpu.make_async_copy(cat_ref.at[part], c_ref.at[part], sem.at[i]))
        copies[-1].start()
    acc_ref[...] = jnp.zeros_like(acc_ref)
    m_ref[...] = jnp.full_like(m_ref, -1e38)
    l_ref[...] = jnp.zeros_like(l_ref)
    u_copy.wait()
    for i in range(n):
        copies[i].wait()
        c = c_ref[i * tile : (i + 1) * tile]
        for b in range(rows // rb):
            sl = slice(b * rb, (b + 1) * rb)
            r = lax.dot_general(u_ref[sl], c, NT, preferred_element_type=f32)
            m_old = m_ref[sl]
            m_new = jnp.maximum(m_old, jnp.max(r, axis=1, keepdims=True))
            alpha = exp_of(m_old - m_new)
            m_ref[sl] = m_new
            total = l_ref[sl] * alpha
            ps = []
            for j in range(tile // 128):
                p = exp_of(r[:, j * 128 : (j + 1) * 128] - m_new)
                total = total + p
                ps.append(p.astype(bf16))
            l_ref[sl] = total
            wide = jnp.concatenate([alpha] * (width // 128), axis=1)
            acc_ref[sl] = acc_ref[sl] * wide + jnp.dot(
                jnp.concatenate(ps, axis=1), c, preferred_element_type=f32
            )
    for b in range(rows // 128):
        sl = slice(b * 128, (b + 1) * 128)
        total = jnp.sum(l_ref[sl], axis=1, keepdims=True)
        acc_ref[sl] = acc_ref[sl] * (1.0 / total)
        st_ref[b : b + 1] = m_ref[sl].T[0:1] + sharpness_divisor * jnp.log(as_row(total))
    every_ref[...] = jnp.broadcast_to(st_ref[...][None], every_ref.shape)
    x = chunk_id()
    chunk = rows // 4
    for k, out_ref in enumerate(out_refs):
        part = pl.ds(pl.multiple_of((x ^ k) * chunk, chunk), chunk)
        out_ref[...] = acc_ref[part, :].astype(bf16)


def pass1(users, catalog, tile=2048, rb=256):
    rows, width = users.shape
    count = catalog.shape[0]
    return pl.pallas_call(
        functools.partial(pass1_kernel, tile, rb),
        in_specs=[HBM, HBM],
        out_specs=[VMEM] * 5,
        out_shape=[struct(rows // 4, width, dtype=bf16)] * 4 + [struct(128, rows // 128, 128)],
        scratch_shapes=[
            pltpu.VMEM((rows, width), bf16),
            pltpu.VMEM((count, width), bf16),
            pltpu.VMEM((rows, width), f32),
            pltpu.VMEM((rows, 128), f32),
            pltpu.VMEM((rows, 128), f32),
            pltpu.VMEM((rows // 128, 128), f32),
            pltpu.SemaphoreType.DMA((count // tile,)),
            pltpu.SemaphoreType.DMA(()),
        ],
        cost_estimate=pl.CostEstimate(
            flops=4 * rows * count * width, bytes_accessed=2 * count * width, transcendentals=rows * count
        ),
        compiler_params=pltpu.CompilerParams(vmem_limit_bytes=20 * MIB),
        name="pass1",
    )(far(users), far(catalog))


def hits_kernel(pos_ref, u_ref, cat_ref, *refs):
    out_refs, own_ref, (hit_ref, sp_ref, c_ref, found_ref, sem) = refs[:4], refs[4], refs[5:]
    items = own_ref.shape[0]
    rows, width = u_ref.shape
    count = cat_ref.shape[0]
    x, shard = chunk_id(), lax.axis_index(ITEM)
    whole_copy = pltpu.make_async_copy(cat_ref, c_ref, sem.at[0])
    whole_copy.start()
    mine = pl.ds(pl.multiple_of(lax.axis_index(USER) * items, items), items)
    own_copy = pltpu.make_async_copy(cat_ref.at[mine], own_ref, sem.at[1])
    own_copy.start()
    hit_ref[...] = jnp.zeros_like(hit_ref)
    base = shard * count
    bits = count.bit_length() - 1

    def scan(g, n):
        for j in range(16):
            found_ref[n] = g * 16 + j
            n = n + ((pos_ref[g * 16 + j] >> bits) == shard).astype(jnp.int32)
        return n

    n_found = lax.fori_loop(0, rows // 16, scan, jnp.int32(0))
    whole_copy.wait()

    @pl.loop(0, n_found)
    def _(i):
        user = found_ref[i]
        here = pos_ref[user] - base
        group = c_ref[pl.ds(pl.multiple_of((here >> 4) << 4, 16), 16), :].astype(f32)
        inside = lax.broadcasted_iota(jnp.int32, group.shape, 0) == (here & 15)
        hit_ref[pl.ds(user, 1), :] = jnp.sum(jnp.where(inside, group, 0.0), axis=0, keepdims=True)

    for b in range(rows // 128):
        sl = slice(b * 128, (b + 1) * 128)
        score = jnp.sum(hit_ref[sl] * u_ref[sl].astype(f32), axis=1, keepdims=True)
        sp_ref[b : b + 1] = as_row(score)
    chunk = rows // 4
    for k, out_ref in enumerate(out_refs):
        part = pl.ds(pl.multiple_of((x ^ k) * chunk, chunk), chunk)
        out_ref[0:chunk] = hit_ref[part, :].astype(bf16)
        rest = jnp.concatenate([sp_ref[pl.ds((x ^ k) * 2 + h, 1), :] for h in range(2)], axis=1)
        terms = []
        for _ in range(3):
            term = rest.astype(bf16).astype(f32)
            rest = rest - term
            terms.append(term)
        terms.append(jnp.zeros((13, width), f32))
        out_ref[chunk:] = jnp.concatenate(terms, axis=0).astype(bf16)
    own_copy.wait()


def find_hits(positives, users, catalog):
    rows, width = users.shape
    count = catalog.shape[0]
    return pl.pallas_call(
        hits_kernel,
        in_specs=[SMEM, VMEM, HBM],
        out_specs=[VMEM] * 5,
        out_shape=[struct(rows // 4 + 16, width, dtype=bf16)] * 4 + [struct(count // 4, width, dtype=bf16)],
        scratch_shapes=[
            pltpu.VMEM((rows, width), f32),
            pltpu.VMEM((rows // 128, 128), f32),
            pltpu.VMEM((count, width), bf16),
            pltpu.SMEM((rows,), jnp.int32),
            pltpu.SemaphoreType.DMA((2,)),
        ],
        cost_estimate=pl.CostEstimate(
            flops=rows * count * width // 2, bytes_accessed=2 * count * width, transcendentals=0
        ),
        compiler_params=pltpu.CompilerParams(vmem_limit_bytes=12 * MIB),
        name="hits",
    )(positives, users, far(catalog))


def combine_kernel(all_ref, *refs):
    u_refs, h_refs, l_refs, out_ref = refs[:4], refs[4:8], refs[8:12], refs[12]
    x, member, shard = chunk_id(), lax.axis_index(USER), lax.axis_index(ITEM)
    shards = all_ref.shape[0] // 4
    chunk, width = u_refs[0].shape
    for k, l_ref in enumerate(l_refs):
        stats = all_ref[pl.ds((member ^ k) * shards, shards)]
        top = jnp.max(stats, axis=0)
        l_ref[...] = top + sharpness_divisor * jnp.log(jnp.sum(exp_of(stats - top[None]), axis=0))
    for h in range(chunk // 128):
        sl = slice(h * 128, (h + 1) * 128)
        row = pl.ds(x * 2 + h, 1)
        total = jnp.zeros((128, width), f32)
        for k in range(4):
            weight = exp_of(all_ref[member * shards + (shard ^ NEAR[k]), row, :] - l_refs[0][row, :])
            wide = jnp.concatenate([as_column(weight)] * (width // 128), axis=1)
            total = total + wide * u_refs[k][sl].astype(f32) - h_refs[k][sl].astype(f32)
        out_ref[sl] = (total / sharpness_divisor).astype(bf16)
    scores = [h_ref[chunk:].astype(f32) for h_ref in h_refs]
    out_ref[chunk:] = ((scores[0] + scores[1]) + (scores[2] + scores[3])).astype(bf16)


def combine(every, us, hs):
    rows, width = hs[0].shape
    return pl.pallas_call(
        combine_kernel,
        in_specs=[VMEM] * 9,
        out_specs=[VMEM] * 5,
        out_shape=[struct(*every.shape[1:])] * 4 + [struct(rows, width, dtype=bf16)],
        compiler_params=pltpu.CompilerParams(vmem_limit_bytes=8 * MIB),
        name="combine",
    )(*near([every, *us, *hs]))


def finish_kernel(lse_ref, *refs):
    parts, out_ref, loss_ref = refs[:4], refs[4], refs[5]
    x = chunk_id()
    chunk = out_ref.shape[0] // 4
    for k, part in enumerate(parts):
        out_ref[pl.ds(pl.multiple_of((x ^ k) * chunk, chunk), chunk), :] = part[0:chunk]
        terms = part[chunk:].astype(f32)
        score = terms[0:1] + terms[1:2] + terms[2:3]
        for h in range(2):
            row = pl.ds((x ^ k) * 2 + h, 1)
            loss_ref[row, :] = (lse_ref[row, :] - score[:, h * 128 : (h + 1) * 128]) / sharpness_divisor


def finish(lse4, parts, rows):
    width = parts[0].shape[1]
    return pl.pallas_call(
        finish_kernel,
        in_specs=[VMEM] * 5,
        out_specs=[VMEM] * 2,
        out_shape=[struct(rows, width, dtype=bf16), struct(rows // 128, 128)],
        compiler_params=pltpu.CompilerParams(vmem_limit_bytes=6 * MIB),
        name="finish",
    )(*near([lse4, *parts]))


def pass2_kernel(tile, lead, n, c_ref, *refs):
    us, infos, poss, (out_ref, tile_ref, sem) = refs[:4], refs[4:8], refs[8:12], refs[-3:]
    member, shard = lax.axis_index(USER), lax.axis_index(ITEM)
    items = c_ref.shape[0]
    copies = []
    for i in range(n):
        start = (lead + i) * tile
        c = c_ref[start : start + tile]
        item = lax.broadcasted_iota(jnp.int32, (tile, 128), 0) + (shard * 4 + member) * items + start
        total = jnp.zeros((tile, c.shape[1]), f32)
        for u_ref, info_ref, pos_ref in zip(us, infos, poss):
            u = u_ref[...]
            r = lax.dot_general(c, u, NT, preferred_element_type=f32)
            ws = []
            for j in range(u.shape[0] // 128):
                w = exp_of(r[:, j * 128 : (j + 1) * 128] - info_ref[j : j + 1])
                ws.append(jnp.where(pos_ref[j : j + 1] == item, w - 1.0, w).astype(bf16))
            total = total + jnp.dot(jnp.concatenate(ws, axis=1), u, preferred_element_type=f32)
        tile_ref[i] = (total / sharpness_divisor).astype(bf16)
        copies.append(pltpu.make_async_copy(tile_ref.at[i], out_ref.at[pl.ds(start, tile)], sem.at[i]))
        copies[-1].start()
    for copy in copies:
        copy.wait()


def pass2(own, us, infos, poss, start, stop, before, tile=512):
    items, width = own.shape
    rows = us[0].shape[0]
    n = (stop - start) // tile
    in_specs = [VMEM] * 13
    args = near([own, *us, *infos, *poss])
    aliases = {}
    if before is not None:
        in_specs.append(HBM)
        aliases = {len(args): 0}
        args.append(before)
    return pl.pallas_call(
        functools.partial(pass2_kernel, tile, start // tile, n),
        in_specs=in_specs,
        out_specs=HBM,
        out_shape=struct(items, width, dtype=bf16),
        scratch_shapes=[pltpu.VMEM((n, tile, width), bf16), pltpu.SemaphoreType.DMA((n,))],
        input_output_aliases=aliases,
        cost_estimate=pl.CostEstimate(
            flops=16 * rows * (stop - start) * width,
            bytes_accessed=8 * rows * width,
            transcendentals=4 * rows * (stop - start),
        ),
        compiler_params=pltpu.CompilerParams(vmem_limit_bytes=14 * MIB),
        name="pass2",
    )(*args)


def swap(x, axis, size, k, mask=None):
    return lax.ppermute(x, axis, [(i, i ^ (k if mask is None else mask)) for i in range(size)])


def exchange(xs, masks):
    return [xs[0]] + [swap(xs[k], ITEM, 32, k, masks[k]) for k in (1, 2, 3)]


def add_kernel(*refs):
    a, out_ref = [ref[...].astype(f32) for ref in refs[:-1]], refs[-1]
    total = (a[0] + a[1]) + (a[2] + a[3]) if len(a) == 4 else a[0] + a[1]
    out_ref[...] = total.astype(out_ref.dtype)


def add(parts, dtype):
    return pl.pallas_call(
        add_kernel,
        in_specs=[VMEM] * len(parts),
        out_specs=VMEM,
        out_shape=struct(*parts[0].shape, dtype=dtype),
        compiler_params=pltpu.CompilerParams(vmem_limit_bytes=4 * MIB),
        name="add",
    )(*near(parts))


def per_device(users, catalog, positives):
    rows = users.shape[0]
    items = catalog.shape[0] // 4
    pos = positives.reshape(rows // 128, 128)
    over = swap(users, USER, 4, 2)
    us = [users, swap(users, USER, 4, 1), over, swap(over, USER, 4, 1)]
    poss = [pos] + [swap(pos, USER, 4, k) for k in (1, 2, 3)]
    *pieces, every = pass1(users, catalog)
    every = lax.all_to_all(every, USER + ITEM, 0, 0, tiled=True)
    *hits, own = find_hits(positives, users, catalog)
    pieces = exchange(pieces, NEAR)
    hits = exchange(hits, NEAR)
    *infos, value = combine(every, pieces, hits)

    a = exchange([value] * 4, REST)
    item_grad = pass2(own, us, infos, poss, 0, SPLIT[0], None)
    value = add(a, f32)
    other = swap(value, ITEM, 32, 1, ACROSS)
    item_grad = pass2(own, us, infos, poss, SPLIT[0], SPLIT[1], item_grad)
    value = add([value, other], bf16)
    got = exchange([value] * 4, NEAR)
    item_grad = pass2(own, us, infos, poss, SPLIT[1], items, item_grad)
    user_grad, loss = finish(infos[0], got, rows)
    return loss.reshape(rows), user_grad, item_grad


SPLIT = (512, 1024)


def solution(mesh):
    grid = Mesh(mesh.devices.reshape(2, 2, 4, 2, 4), USER + ITEM)

    return jax.shard_map(
        per_device,
        mesh=grid,
        in_specs=(P(USER, None), P(ITEM, None), P(USER)),
        out_specs=(P(USER), P(USER, None), P(ITEM + USER, None)),
        check_vma=False,
    )
```

```python
import functools
import math

import jax
import jax.numpy as jnp
from jax import lax
from jax.experimental import pallas as pl
from jax.experimental.pallas import tpu as pltpu
from jax.sharding import Mesh
from jax.sharding import PartitionSpec as P

sharpness_divisor = 4.0
SCALE = math.log2(math.e) / sharpness_divisor
NT = (((1,), (1,)), ((), ()))
ITEM = ("z", "y_hi", "x")
USER = ("y_lo", "core")
VMEM = pl.BlockSpec(memory_space=pltpu.VMEM)
SMEM = pl.BlockSpec(memory_space=pltpu.SMEM)
ANY = pl.BlockSpec(memory_space=pl.ANY)
HBM = pl.BlockSpec(memory_space=pltpu.HBM)
f32 = jnp.float32
bf16 = jnp.bfloat16
MIB = 1 << 20


NEAR = (0, 8, 1, 9)
REST = (0, 24, 3, 27)
ACROSS = 4


def chunk_id():
    x, z = lax.axis_index("x"), lax.axis_index("z")
    return ((z ^ (z >> 1)) & 1) + 2 * ((x ^ (x >> 1)) & 1)


def exp_of(x):
    return jnp.exp2(x * SCALE)


def near(xs):
    return [pltpu.with_memory_space_constraint(x, pltpu.VMEM) for x in xs]


def far(x):
    return pltpu.with_memory_space_constraint(x, pltpu.HBM)


def struct(*shape, dtype=f32):
    return jax.ShapeDtypeStruct(shape, dtype)


def as_row(column):
    return jnp.broadcast_to(column, (128, 128)).T[0:1]


def as_column(row):
    return jnp.broadcast_to(row, (128, 128)).T


def pass1_kernel(tile, rb, users_ref, cat_ref, *refs):
    out_refs, every_ref, (u_ref, c_ref, acc_ref, m_ref, l_ref, st_ref, sem, u_sem) = refs[:4], refs[4], refs[5:]
    rows = u_ref.shape[0]
    u_copy = pltpu.make_async_copy(users_ref, u_ref, u_sem)
    u_copy.start()
    count, width = cat_ref.shape
    n = count // tile
    copies = []
    for i in range(n):
        part = pl.ds(i * tile, tile)
        copies.append(pltpu.make_async_copy(cat_ref.at[part], c_ref.at[part], sem.at[i]))
        copies[-1].start()
    acc_ref[...] = jnp.zeros_like(acc_ref)
    m_ref[...] = jnp.full_like(m_ref, -1e38)
    l_ref[...] = jnp.zeros_like(l_ref)
    u_copy.wait()
    for i in range(n):
        copies[i].wait()
        c = c_ref[i * tile : (i + 1) * tile]
        for b in range(rows // rb):
            sl = slice(b * rb, (b + 1) * rb)
            r = lax.dot_general(u_ref[sl], c, NT, preferred_element_type=f32)
            m_old = m_ref[sl]
            m_new = jnp.maximum(m_old, jnp.max(r, axis=1, keepdims=True))
            alpha = exp_of(m_old - m_new)
            m_ref[sl] = m_new
            total = l_ref[sl] * alpha
            ps = []
            for j in range(tile // 128):
                p = exp_of(r[:, j * 128 : (j + 1) * 128] - m_new)
                total = total + p
                ps.append(p.astype(bf16))
            l_ref[sl] = total
            wide = jnp.concatenate([alpha] * (width // 128), axis=1)
            acc_ref[sl] = acc_ref[sl] * wide + jnp.dot(
                jnp.concatenate(ps, axis=1), c, preferred_element_type=f32
            )
    for b in range(rows // 128):
        sl = slice(b * 128, (b + 1) * 128)
        total = jnp.sum(l_ref[sl], axis=1, keepdims=True)
        acc_ref[sl] = acc_ref[sl] * (1.0 / total)
        st_ref[b : b + 1] = m_ref[sl].T[0:1] + sharpness_divisor * jnp.log(as_row(total))
    every_ref[...] = jnp.broadcast_to(st_ref[...][None], every_ref.shape)
    x = chunk_id()
    chunk = rows // 4
    for k, out_ref in enumerate(out_refs):
        part = pl.ds(pl.multiple_of((x ^ k) * chunk, chunk), chunk)
        out_ref[...] = acc_ref[part, :].astype(bf16)


def pass1(users, catalog, tile=2048, rb=256):
    rows, width = users.shape
    count = catalog.shape[0]
    return pl.pallas_call(
        functools.partial(pass1_kernel, tile, rb),
        in_specs=[HBM, HBM],
        out_specs=[VMEM] * 5,
        out_shape=[struct(rows // 4, width, dtype=bf16)] * 4 + [struct(128, rows // 128, 128)],
        scratch_shapes=[
            pltpu.VMEM((rows, width), bf16),
            pltpu.VMEM((count, width), bf16),
            pltpu.VMEM((rows, width), f32),
            pltpu.VMEM((rows, 128), f32),
            pltpu.VMEM((rows, 128), f32),
            pltpu.VMEM((rows // 128, 128), f32),
            pltpu.SemaphoreType.DMA((count // tile,)),
            pltpu.SemaphoreType.DMA(()),
        ],
        cost_estimate=pl.CostEstimate(
            flops=4 * rows * count * width, bytes_accessed=2 * count * width, transcendentals=rows * count
        ),
        compiler_params=pltpu.CompilerParams(vmem_limit_bytes=20 * MIB),
        name="pass1",
    )(far(users), far(catalog))


def hits_kernel(pos_ref, u_ref, cat_ref, *refs):
    out_refs, own_ref, (hit_ref, sp_ref, c_ref, found_ref, sem) = refs[:4], refs[4], refs[5:]
    items = own_ref.shape[0]
    rows, width = u_ref.shape
    count = cat_ref.shape[0]
    x, shard = chunk_id(), lax.axis_index(ITEM)
    whole_copy = pltpu.make_async_copy(cat_ref, c_ref, sem.at[0])
    whole_copy.start()
    mine = pl.ds(pl.multiple_of(lax.axis_index(USER) * items, items), items)
    own_copy = pltpu.make_async_copy(cat_ref.at[mine], own_ref, sem.at[1])
    own_copy.start()
    hit_ref[...] = jnp.zeros_like(hit_ref)
    base = shard * count
    bits = count.bit_length() - 1

    def scan(g, n):
        for j in range(16):
            found_ref[n] = g * 16 + j
            n = n + ((pos_ref[g * 16 + j] >> bits) == shard).astype(jnp.int32)
        return n

    n_found = lax.fori_loop(0, rows // 16, scan, jnp.int32(0))
    whole_copy.wait()

    @pl.loop(0, n_found)
    def _(i):
        user = found_ref[i]
        here = pos_ref[user] - base
        group = c_ref[pl.ds(pl.multiple_of((here >> 4) << 4, 16), 16), :].astype(f32)
        inside = lax.broadcasted_iota(jnp.int32, group.shape, 0) == (here & 15)
        hit_ref[pl.ds(user, 1), :] = jnp.sum(jnp.where(inside, group, 0.0), axis=0, keepdims=True)

    for b in range(rows // 128):
        sl = slice(b * 128, (b + 1) * 128)
        score = jnp.sum(hit_ref[sl] * u_ref[sl].astype(f32), axis=1, keepdims=True)
        sp_ref[b : b + 1] = as_row(score)
    chunk = rows // 4
    for k, out_ref in enumerate(out_refs):
        part = pl.ds(pl.multiple_of((x ^ k) * chunk, chunk), chunk)
        out_ref[0:chunk] = hit_ref[part, :].astype(bf16)
        rest = jnp.concatenate([sp_ref[pl.ds((x ^ k) * 2 + h, 1), :] for h in range(2)], axis=1)
        terms = []
        for _ in range(3):
            term = rest.astype(bf16).astype(f32)
            rest = rest - term
            terms.append(term)
        terms.append(jnp.zeros((13, width), f32))
        out_ref[chunk:] = jnp.concatenate(terms, axis=0).astype(bf16)
    own_copy.wait()


def find_hits(positives, users, catalog):
    rows, width = users.shape
    count = catalog.shape[0]
    return pl.pallas_call(
        hits_kernel,
        in_specs=[SMEM, VMEM, HBM],
        out_specs=[VMEM] * 5,
        out_shape=[struct(rows // 4 + 16, width, dtype=bf16)] * 4 + [struct(count // 4, width, dtype=bf16)],
        scratch_shapes=[
            pltpu.VMEM((rows, width), f32),
            pltpu.VMEM((rows // 128, 128), f32),
            pltpu.VMEM((count, width), bf16),
            pltpu.SMEM((rows,), jnp.int32),
            pltpu.SemaphoreType.DMA((2,)),
        ],
        cost_estimate=pl.CostEstimate(
            flops=rows * count * width // 2, bytes_accessed=2 * count * width, transcendentals=0
        ),
        compiler_params=pltpu.CompilerParams(vmem_limit_bytes=12 * MIB),
        name="hits",
    )(positives, users, far(catalog))


def combine_kernel(all_ref, *refs):
    u_refs, h_refs, l_refs, out_ref = refs[:4], refs[4:8], refs[8:12], refs[12]
    x, member, shard = chunk_id(), lax.axis_index(USER), lax.axis_index(ITEM)
    shards = all_ref.shape[0] // 4
    chunk, width = u_refs[0].shape
    for k, l_ref in enumerate(l_refs):
        stats = all_ref[pl.ds((member ^ k) * shards, shards)]
        top = jnp.max(stats, axis=0)
        l_ref[...] = top + sharpness_divisor * jnp.log(jnp.sum(exp_of(stats - top[None]), axis=0))
    for h in range(chunk // 128):
        sl = slice(h * 128, (h + 1) * 128)
        row = pl.ds(x * 2 + h, 1)
        total = jnp.zeros((128, width), f32)
        for k in range(4):
            weight = exp_of(all_ref[member * shards + (shard ^ NEAR[k]), row, :] - l_refs[0][row, :])
            wide = jnp.concatenate([as_column(weight)] * (width // 128), axis=1)
            total = total + wide * u_refs[k][sl].astype(f32) - h_refs[k][sl].astype(f32)
        out_ref[sl] = (total / sharpness_divisor).astype(bf16)
    scores = [h_ref[chunk:].astype(f32) for h_ref in h_refs]
    out_ref[chunk:] = ((scores[0] + scores[1]) + (scores[2] + scores[3])).astype(bf16)


def combine(every, us, hs):
    rows, width = hs[0].shape
    return pl.pallas_call(
        combine_kernel,
        in_specs=[VMEM] * 9,
        out_specs=[VMEM] * 5,
        out_shape=[struct(*every.shape[1:])] * 4 + [struct(rows, width, dtype=bf16)],
        compiler_params=pltpu.CompilerParams(vmem_limit_bytes=8 * MIB),
        name="combine",
    )(*near([every, *us, *hs]))


def finish_kernel(lse_ref, *refs):
    parts, out_ref, loss_ref = refs[:4], refs[4], refs[5]
    x = chunk_id()
    chunk = out_ref.shape[0] // 4
    for k, part in enumerate(parts):
        out_ref[pl.ds(pl.multiple_of((x ^ k) * chunk, chunk), chunk), :] = part[0:chunk]
        terms = part[chunk:].astype(f32)
        score = terms[0:1] + terms[1:2] + terms[2:3]
        for h in range(2):
            row = pl.ds((x ^ k) * 2 + h, 1)
            loss_ref[row, :] = (lse_ref[row, :] - score[:, h * 128 : (h + 1) * 128]) / sharpness_divisor


def finish(lse4, parts, rows):
    width = parts[0].shape[1]
    return pl.pallas_call(
        finish_kernel,
        in_specs=[VMEM] * 5,
        out_specs=[VMEM] * 2,
        out_shape=[struct(rows, width, dtype=bf16), struct(rows // 128, 128)],
        compiler_params=pltpu.CompilerParams(vmem_limit_bytes=6 * MIB),
        name="finish",
    )(*near([lse4, *parts]))


def pass2_kernel(tile, lead, n, c_ref, *refs):
    us, infos, poss, (out_ref, tile_ref, sem) = refs[:4], refs[4:8], refs[8:12], refs[-3:]
    member, shard = lax.axis_index(USER), lax.axis_index(ITEM)
    items = c_ref.shape[0]
    copies = []
    for i in range(n):
        start = (lead + i) * tile
        c = c_ref[start : start + tile]
        item = lax.broadcasted_iota(jnp.int32, (tile, 128), 0) + (shard * 4 + member) * items + start
        total = jnp.zeros((tile, c.shape[1]), f32)
        for u_ref, info_ref, pos_ref in zip(us, infos, poss):
            u = u_ref[...]
            r = lax.dot_general(c, u, NT, preferred_element_type=f32)
            ws = []
            for j in range(u.shape[0] // 128):
                w = exp_of(r[:, j * 128 : (j + 1) * 128] - info_ref[j : j + 1])
                ws.append(jnp.where(pos_ref[j : j + 1] == item, w - 1.0, w).astype(bf16))
            total = total + jnp.dot(jnp.concatenate(ws, axis=1), u, preferred_element_type=f32)
        tile_ref[i] = (total / sharpness_divisor).astype(bf16)
        copies.append(pltpu.make_async_copy(tile_ref.at[i], out_ref.at[pl.ds(start, tile)], sem.at[i]))
        copies[-1].start()
    for copy in copies:
        copy.wait()


def pass2(own, us, infos, poss, start, stop, before, tile=512):
    items, width = own.shape
    rows = us[0].shape[0]
    n = (stop - start) // tile
    in_specs = [VMEM] * 13
    args = near([own, *us, *infos, *poss])
    aliases = {}
    if before is not None:
        in_specs.append(HBM)
        aliases = {len(args): 0}
        args.append(before)
    return pl.pallas_call(
        functools.partial(pass2_kernel, tile, start // tile, n),
        in_specs=in_specs,
        out_specs=HBM,
        out_shape=struct(items, width, dtype=bf16),
        scratch_shapes=[pltpu.VMEM((n, tile, width), bf16), pltpu.SemaphoreType.DMA((n,))],
        input_output_aliases=aliases,
        cost_estimate=pl.CostEstimate(
            flops=16 * rows * (stop - start) * width,
            bytes_accessed=8 * rows * width,
            transcendentals=4 * rows * (stop - start),
        ),
        compiler_params=pltpu.CompilerParams(vmem_limit_bytes=14 * MIB),
        name="pass2",
    )(*args)


def swap(x, axis, size, k, mask=None):
    return lax.ppermute(x, axis, [(i, i ^ (k if mask is None else mask)) for i in range(size)])


def exchange(xs, masks):
    return [xs[0]] + [swap(xs[k], ITEM, 32, k, masks[k]) for k in (1, 2, 3)]


def add_kernel(*refs):
    a, out_ref = [ref[...].astype(f32) for ref in refs[:-1]], refs[-1]
    total = (a[0] + a[1]) + (a[2] + a[3]) if len(a) == 4 else a[0] + a[1]
    out_ref[...] = total.astype(out_ref.dtype)


def add(parts, dtype):
    return pl.pallas_call(
        add_kernel,
        in_specs=[VMEM] * len(parts),
        out_specs=VMEM,
        out_shape=struct(*parts[0].shape, dtype=dtype),
        compiler_params=pltpu.CompilerParams(vmem_limit_bytes=4 * MIB),
        name="add",
    )(*near(parts))


def per_device(users, catalog, positives):
    rows = users.shape[0]
    items = catalog.shape[0] // 4
    pos = positives.reshape(rows // 128, 128)
    over = swap(users, USER, 4, 2)
    us = [users, swap(users, USER, 4, 1), over, swap(over, USER, 4, 1)]
    poss = [pos] + [swap(pos, USER, 4, k) for k in (1, 2, 3)]
    *pieces, every = pass1(users, catalog)
    every = lax.all_to_all(every, USER + ITEM, 0, 0, tiled=True)
    *hits, own = find_hits(positives, users, catalog)
    pieces = exchange(pieces, NEAR)
    hits = exchange(hits, NEAR)
    *infos, value = combine(every, pieces, hits)

    a = exchange([value] * 4, REST)
    item_grad = pass2(own, us, infos, poss, 0, SPLIT[0], None)
    value = add(a, f32)
    other = swap(value, ITEM, 32, 1, ACROSS)
    item_grad = pass2(own, us, infos, poss, SPLIT[0], SPLIT[1], item_grad)
    value = add([value, other], bf16)
    got = exchange([value] * 4, NEAR)
    item_grad = pass2(own, us, infos, poss, SPLIT[1], items, item_grad)
    user_grad, loss = finish(infos[0], got, rows)
    return loss.reshape(rows), user_grad, item_grad


SPLIT = (512, 1024)


def solution(mesh):
    grid = Mesh(mesh.devices.reshape(2, 2, 4, 2, 4), USER + ITEM)

    return jax.shard_map(
        per_device,
        mesh=grid,
        in_specs=(P(USER, None), P(ITEM, None), P(USER)),
        out_specs=(P(USER), P(USER, None), P(ITEM + USER, None)),
        check_vma=False,
    )
```

```python
import functools
import math

import jax
import jax.numpy as jnp
from jax import lax
from jax.experimental import pallas as pl
from jax.experimental.pallas import tpu as pltpu
from jax.sharding import Mesh
from jax.sharding import PartitionSpec as P

sharpness_divisor = 4.0
SCALE = math.log2(math.e) / sharpness_divisor
NT = (((1,), (1,)), ((), ()))
ITEM = ("z", "y_hi", "x")
USER = ("y_lo", "core")
VMEM = pl.BlockSpec(memory_space=pltpu.VMEM)
SMEM = pl.BlockSpec(memory_space=pltpu.SMEM)
ANY = pl.BlockSpec(memory_space=pl.ANY)
HBM = pl.BlockSpec(memory_space=pltpu.HBM)
f32 = jnp.float32
bf16 = jnp.bfloat16
MIB = 1 << 20


NEAR = (0, 8, 1, 9)
REST = (0, 24, 3, 27)
ACROSS = 4


def chunk_id():
    x, z = lax.axis_index("x"), lax.axis_index("z")
    return ((z ^ (z >> 1)) & 1) + 2 * ((x ^ (x >> 1)) & 1)


def exp_of(x):
    return jnp.exp2(x * SCALE)


def near(xs):
    return [pltpu.with_memory_space_constraint(x, pltpu.VMEM) for x in xs]


def far(x):
    return pltpu.with_memory_space_constraint(x, pltpu.HBM)


def struct(*shape, dtype=f32):
    return jax.ShapeDtypeStruct(shape, dtype)


def as_row(column):
    return jnp.broadcast_to(column, (128, 128)).T[0:1]


def as_column(row):
    return jnp.broadcast_to(row, (128, 128)).T


def pass1_kernel(tile, rb, users_ref, cat_ref, *refs):
    out_refs, every_ref, (u_ref, c_ref, acc_ref, m_ref, l_ref, st_ref, sem, u_sem) = refs[:4], refs[4], refs[5:]
    rows = u_ref.shape[0]
    u_copy = pltpu.make_async_copy(users_ref, u_ref, u_sem)
    u_copy.start()
    count, width = cat_ref.shape
    n = count // tile
    copies = []
    for i in range(n):
        part = pl.ds(i * tile, tile)
        copies.append(pltpu.make_async_copy(cat_ref.at[part], c_ref.at[part], sem.at[i]))
        copies[-1].start()
    acc_ref[...] = jnp.zeros_like(acc_ref)
    m_ref[...] = jnp.full_like(m_ref, -1e38)
    l_ref[...] = jnp.zeros_like(l_ref)
    u_copy.wait()
    for i in range(n):
        copies[i].wait()
        c = c_ref[i * tile : (i + 1) * tile]
        for b in range(rows // rb):
            sl = slice(b * rb, (b + 1) * rb)
            r = lax.dot_general(u_ref[sl], c, NT, preferred_element_type=f32)
            m_old = m_ref[sl]
            m_new = jnp.maximum(m_old, jnp.max(r, axis=1, keepdims=True))
            alpha = exp_of(m_old - m_new)
            m_ref[sl] = m_new
            total = l_ref[sl] * alpha
            ps = []
            for j in range(tile // 128):
                p = exp_of(r[:, j * 128 : (j + 1) * 128] - m_new)
                total = total + p
                ps.append(p.astype(bf16))
            l_ref[sl] = total
            wide = jnp.concatenate([alpha] * (width // 128), axis=1)
            acc_ref[sl] = acc_ref[sl] * wide + jnp.dot(
                jnp.concatenate(ps, axis=1), c, preferred_element_type=f32
            )
    for b in range(rows // 128):
        sl = slice(b * 128, (b + 1) * 128)
        total = jnp.sum(l_ref[sl], axis=1, keepdims=True)
        acc_ref[sl] = acc_ref[sl] * (1.0 / total)
        st_ref[b : b + 1] = m_ref[sl].T[0:1] + sharpness_divisor * jnp.log(as_row(total))
    every_ref[...] = jnp.broadcast_to(st_ref[...][None], every_ref.shape)
    x = chunk_id()
    chunk = rows // 4
    for k, out_ref in enumerate(out_refs):
        part = pl.ds(pl.multiple_of((x ^ k) * chunk, chunk), chunk)
        out_ref[...] = acc_ref[part, :].astype(bf16)


def pass1(users, catalog, tile=2048, rb=256):
    rows, width = users.shape
    count = catalog.shape[0]
    return pl.pallas_call(
        functools.partial(pass1_kernel, tile, rb),
        in_specs=[HBM, HBM],
        out_specs=[VMEM] * 5,
        out_shape=[struct(rows // 4, width, dtype=bf16)] * 4 + [struct(128, rows // 128, 128)],
        scratch_shapes=[
            pltpu.VMEM((rows, width), bf16),
            pltpu.VMEM((count, width), bf16),
            pltpu.VMEM((rows, width), f32),
            pltpu.VMEM((rows, 128), f32),
            pltpu.VMEM((rows, 128), f32),
            pltpu.VMEM((rows // 128, 128), f32),
            pltpu.SemaphoreType.DMA((count // tile,)),
            pltpu.SemaphoreType.DMA(()),
        ],
        cost_estimate=pl.CostEstimate(
            flops=4 * rows * count * width, bytes_accessed=2 * count * width, transcendentals=rows * count
        ),
        compiler_params=pltpu.CompilerParams(vmem_limit_bytes=20 * MIB),
        name="pass1",
    )(far(users), far(catalog))


def hits_kernel(pos_ref, u_ref, cat_ref, *refs):
    out_refs, (hit_ref, sp_ref, c_ref, found_ref, sem) = refs[:4], refs[4:]
    rows, width = u_ref.shape
    count = cat_ref.shape[0]
    x, shard = chunk_id(), lax.axis_index(ITEM)
    whole_copy = pltpu.make_async_copy(cat_ref, c_ref, sem)
    whole_copy.start()
    hit_ref[...] = jnp.zeros_like(hit_ref)
    base = shard * count
    bits = count.bit_length() - 1

    def scan(g, n):
        for j in range(16):
            found_ref[n] = g * 16 + j
            n = n + ((pos_ref[g * 16 + j] >> bits) == shard).astype(jnp.int32)
        return n

    n_found = lax.fori_loop(0, rows // 16, scan, jnp.int32(0))
    whole_copy.wait()

    @pl.loop(0, n_found)
    def _(i):
        user = found_ref[i]
        here = pos_ref[user] - base
        group = c_ref[pl.ds(pl.multiple_of((here >> 4) << 4, 16), 16), :].astype(f32)
        inside = lax.broadcasted_iota(jnp.int32, group.shape, 0) == (here & 15)
        hit_ref[pl.ds(user, 1), :] = jnp.sum(jnp.where(inside, group, 0.0), axis=0, keepdims=True)

    for b in range(rows // 128):
        sl = slice(b * 128, (b + 1) * 128)
        score = jnp.sum(hit_ref[sl] * u_ref[sl].astype(f32), axis=1, keepdims=True)
        sp_ref[b : b + 1] = as_row(score)
    chunk = rows // 4
    for k, out_ref in enumerate(out_refs):
        part = pl.ds(pl.multiple_of((x ^ k) * chunk, chunk), chunk)
        out_ref[0:chunk] = hit_ref[part, :].astype(bf16)
        rest = jnp.concatenate([sp_ref[pl.ds((x ^ k) * 2 + h, 1), :] for h in range(2)], axis=1)
        terms = []
        for _ in range(3):
            term = rest.astype(bf16).astype(f32)
            rest = rest - term
            terms.append(term)
        terms.append(jnp.zeros((13, width), f32))
        out_ref[chunk:] = jnp.concatenate(terms, axis=0).astype(bf16)


def find_hits(positives, users, catalog):
    rows, width = users.shape
    count = catalog.shape[0]
    return pl.pallas_call(
        hits_kernel,
        in_specs=[SMEM, VMEM, HBM],
        out_specs=[VMEM] * 4,
        out_shape=[struct(rows // 4 + 16, width, dtype=bf16)] * 4,
        scratch_shapes=[
            pltpu.VMEM((rows, width), f32),
            pltpu.VMEM((rows // 128, 128), f32),
            pltpu.VMEM((count, width), bf16),
            pltpu.SMEM((rows,), jnp.int32),
            pltpu.SemaphoreType.DMA(()),
        ],
        cost_estimate=pl.CostEstimate(
            flops=rows * count * width // 2, bytes_accessed=2 * count * width, transcendentals=0
        ),
        compiler_params=pltpu.CompilerParams(vmem_limit_bytes=12 * MIB),
        name="hits",
    )(positives, users, far(catalog))


def combine_kernel(all_ref, *refs):
    u_refs, h_refs, l_refs, out_ref = refs[:4], refs[4:8], refs[8:12], refs[12]
    x, member, shard = chunk_id(), lax.axis_index(USER), lax.axis_index(ITEM)
    shards = all_ref.shape[0] // 4
    chunk, width = u_refs[0].shape
    for k, l_ref in enumerate(l_refs):
        stats = all_ref[pl.ds((member ^ k) * shards, shards)]
        top = jnp.max(stats, axis=0)
        l_ref[...] = top + sharpness_divisor * jnp.log(jnp.sum(exp_of(stats - top[None]), axis=0))
    for h in range(chunk // 128):
        sl = slice(h * 128, (h + 1) * 128)
        row = pl.ds(x * 2 + h, 1)
        total = jnp.zeros((128, width), f32)
        for k in range(4):
            weight = exp_of(all_ref[member * shards + (shard ^ NEAR[k]), row, :] - l_refs[0][row, :])
            wide = jnp.concatenate([as_column(weight)] * (width // 128), axis=1)
            total = total + wide * u_refs[k][sl].astype(f32) - h_refs[k][sl].astype(f32)
        out_ref[sl] = (total / sharpness_divisor).astype(bf16)
    scores = [h_ref[chunk:].astype(f32) for h_ref in h_refs]
    out_ref[chunk:] = ((scores[0] + scores[1]) + (scores[2] + scores[3])).astype(bf16)


def combine(every, us, hs):
    rows, width = hs[0].shape
    return pl.pallas_call(
        combine_kernel,
        in_specs=[VMEM] * 9,
        out_specs=[VMEM] * 5,
        out_shape=[struct(*every.shape[1:])] * 4 + [struct(rows, width, dtype=bf16)],
        compiler_params=pltpu.CompilerParams(vmem_limit_bytes=8 * MIB),
        name="combine",
    )(*near([every, *us, *hs]))


def finish_kernel(lse_ref, *refs):
    parts, out_ref, loss_ref = refs[:4], refs[4], refs[5]
    x = chunk_id()
    chunk = out_ref.shape[0] // 4
    for k, part in enumerate(parts):
        out_ref[pl.ds(pl.multiple_of((x ^ k) * chunk, chunk), chunk), :] = part[0:chunk]
        terms = part[chunk:].astype(f32)
        score = terms[0:1] + terms[1:2] + terms[2:3]
        for h in range(2):
            row = pl.ds((x ^ k) * 2 + h, 1)
            loss_ref[row, :] = (lse_ref[row, :] - score[:, h * 128 : (h + 1) * 128]) / sharpness_divisor


def finish(lse4, parts, rows):
    width = parts[0].shape[1]
    return pl.pallas_call(
        finish_kernel,
        in_specs=[VMEM] * 5,
        out_specs=[VMEM] * 2,
        out_shape=[struct(rows, width, dtype=bf16), struct(rows // 128, 128)],
        compiler_params=pltpu.CompilerParams(vmem_limit_bytes=6 * MIB),
        name="finish",
    )(*near([lse4, *parts]))


def pass2_kernel(tile, lead, n, c_ref, *refs):
    us, infos, poss, (out_ref, tile_ref, sem) = refs[:4], refs[4:8], refs[8:12], refs[-3:]
    member, shard = lax.axis_index(USER), lax.axis_index(ITEM)
    items = c_ref.shape[0]
    copies = []
    for i in range(n):
        start = (lead + i) * tile
        c = c_ref[start : start + tile]
        item = lax.broadcasted_iota(jnp.int32, (tile, 128), 0) + (shard * 4 + member) * items + start
        total = jnp.zeros((tile, c.shape[1]), f32)
        for u_ref, info_ref, pos_ref in zip(us, infos, poss):
            u = u_ref[...]
            r = lax.dot_general(c, u, NT, preferred_element_type=f32)
            ws = []
            for j in range(u.shape[0] // 128):
                w = exp_of(r[:, j * 128 : (j + 1) * 128] - info_ref[j : j + 1])
                ws.append(jnp.where(pos_ref[j : j + 1] == item, w - 1.0, w).astype(bf16))
            total = total + jnp.dot(jnp.concatenate(ws, axis=1), u, preferred_element_type=f32)
        tile_ref[i] = (total / sharpness_divisor).astype(bf16)
        copies.append(pltpu.make_async_copy(tile_ref.at[i], out_ref.at[pl.ds(start, tile)], sem.at[i]))
        copies[-1].start()
    for copy in copies:
        copy.wait()


def pass2(own, us, infos, poss, start, stop, before, tile=512):
    items, width = own.shape
    rows = us[0].shape[0]
    n = (stop - start) // tile
    in_specs = [VMEM] * 13
    args = near([own, *us, *infos, *poss])
    aliases = {}
    if before is not None:
        in_specs.append(HBM)
        aliases = {len(args): 0}
        args.append(before)
    return pl.pallas_call(
        functools.partial(pass2_kernel, tile, start // tile, n),
        in_specs=in_specs,
        out_specs=HBM,
        out_shape=struct(items, width, dtype=bf16),
        scratch_shapes=[pltpu.VMEM((n, tile, width), bf16), pltpu.SemaphoreType.DMA((n,))],
        input_output_aliases=aliases,
        cost_estimate=pl.CostEstimate(
            flops=16 * rows * (stop - start) * width,
            bytes_accessed=8 * rows * width,
            transcendentals=4 * rows * (stop - start),
        ),
        compiler_params=pltpu.CompilerParams(vmem_limit_bytes=14 * MIB),
        name="pass2",
    )(*args)


def hold_kernel(u0, u1, u2, cat_ref, v0, v1, v2, own_ref, sem):
    items = own_ref.shape[0]
    mine = pl.ds(pl.multiple_of(lax.axis_index(USER) * items, items), items)
    own_copy = pltpu.make_async_copy(cat_ref.at[mine], own_ref, sem)
    own_copy.start()
    for u_ref, v_ref in ((u0, v0), (u1, v1), (u2, v2)):
        v_ref[...] = u_ref[...]
    own_copy.wait()


def hold(us, catalog):
    count, width = catalog.shape
    return pl.pallas_call(
        hold_kernel,
        in_specs=[VMEM] * 3 + [HBM],
        out_specs=[VMEM] * 4,
        out_shape=[struct(*u.shape, dtype=u.dtype) for u in us] + [struct(count // 4, width, dtype=bf16)],
        scratch_shapes=[pltpu.SemaphoreType.DMA(())],
        compiler_params=pltpu.CompilerParams(vmem_limit_bytes=6 * MIB),
        name="hold",
    )(*us, far(catalog))


def swap(x, axis, size, k, mask=None):
    return lax.ppermute(x, axis, [(i, i ^ (k if mask is None else mask)) for i in range(size)])


def exchange(xs, masks):
    return [xs[0]] + [swap(xs[k], ITEM, 32, k, masks[k]) for k in (1, 2, 3)]


def add_kernel(*refs):
    a, out_ref = [ref[...].astype(f32) for ref in refs[:-1]], refs[-1]
    total = (a[0] + a[1]) + (a[2] + a[3]) if len(a) == 4 else a[0] + a[1]
    out_ref[...] = total.astype(out_ref.dtype)


def add(parts, dtype):
    return pl.pallas_call(
        add_kernel,
        in_specs=[VMEM] * len(parts),
        out_specs=VMEM,
        out_shape=struct(*parts[0].shape, dtype=dtype),
        compiler_params=pltpu.CompilerParams(vmem_limit_bytes=4 * MIB),
        name="add",
    )(*near(parts))


def per_device(users, catalog, positives):
    rows = users.shape[0]
    items = catalog.shape[0] // 4
    pos = positives.reshape(rows // 128, 128)
    over = swap(users, USER, 4, 2)
    us = [users, swap(users, USER, 4, 1), over, swap(over, USER, 4, 1)]
    poss = [pos] + [swap(pos, USER, 4, k) for k in (1, 2, 3)]
    *pieces, every = pass1(users, catalog)
    every = lax.all_to_all(every, USER + ITEM, 0, 0, tiled=True)
    hits = find_hits(positives, users, catalog)
    pieces = exchange(pieces, NEAR)
    hits = exchange(hits, NEAR)
    *infos, value = combine(every, pieces, hits)

    a = exchange([value] * 4, REST)
    *held, own = hold(us[1:], catalog)
    us = [users, *held]
    item_grad = pass2(own, us, infos, poss, 0, SPLIT[0], None)
    value = add(a, f32)
    other = swap(value, ITEM, 32, 1, ACROSS)
    item_grad = pass2(own, us, infos, poss, SPLIT[0], SPLIT[1], item_grad)
    value = add([value, other], bf16)
    got = exchange([value] * 4, NEAR)
    item_grad = pass2(own, us, infos, poss, SPLIT[1], items, item_grad)
    user_grad, loss = finish(infos[0], got, rows)
    return loss.reshape(rows), user_grad, item_grad


SPLIT = (512, 1024)


def solution(mesh):
    grid = Mesh(mesh.devices.reshape(2, 2, 4, 2, 4), USER + ITEM)

    return jax.shard_map(
        per_device,
        mesh=grid,
        in_specs=(P(USER, None), P(ITEM, None), P(USER)),
        out_specs=(P(USER), P(USER, None), P(ITEM + USER, None)),
        check_vma=False,
    )
```
